256 devices in a mesh: frame: 8 (over z), tile: 32 (over x, y, core).
Axes of the slice: x: 4, y: 4, z: 8, core: 2. Of those that a mesh axis runs over, the one named last changes fastest.
Arguments:
- kspace_samples: bfloat16 [16, 128, 32, 128], P('frame', 'tile'), may hold values from -6 to 6
- density: bfloat16 [16, 128, 128], P('frame', 'tile'), may hold values from 0.796875 to 8
- sample_frac: bfloat16 [16, 128, 3, 128], P('frame', 'tile'), may hold values from 0 to 1
- row_offsets: int32 [16, 128, 128], P('frame', 'tile'), may hold values from 0 to 2
- depth_base: int32 [16, 128, 128], P('frame', 'tile'), may hold values from 0 to 127
- block_base: int32 [16, 128, 2], P('frame', 'tile'), may hold values from 0 to 127, as said below
- coil_maps: bfloat16 [16, 2, 128, 128, 128], P(None, None, 'tile'), may hold values from -1.5 to 1.5
- estimate: float32 [16, 2, 128, 128, 128], P('frame', None, 'tile'), may hold values from -6 to 6
Outputs:
- updated: float32 [16, 2, 128, 128, 128], P('frame', None, 'tile')
The draws below stay inside these ranges and needn't reach their ends.
Inputs may be any that keep to these rules, and one draw needn't show every extreme that they name: `block_base`: block b of a frame is held by tile index b // 4. Its kx planes are xb .. xb + 5 mod 128, and tile number p holds planes p * 4 .. p * 4 + 3. In every frame, at most 1 block of one tile index touch any one tile, and some tile is touched by exactly 1 block of every tile index.
All inputs are finite; a program needn't handle non-finite values.
Results may differ from the reference program's by a relative error of at most 0.0095.
Values may be sent and summed in bfloat16 or wider, within the bound.
A program may use at most 128 MiB of HBM per device.

```python
import math
import jax
import jax.numpy as jnp
from jax import lax

GRID = 128
COILS = 16
BLK_DEV = 4
SAMP = 128
WIN = 8
FRAMES = 16
BLOCKS = 128
CAP = 1
SAMPLES = 16384


def draw_block_base(key, part):
    tile_count = BLOCKS // BLK_DEV
    tile_width = GRID // tile_count
    centre_span = 1 + (tile_width + 4) // tile_width
    region = (tile_count - centre_span) // 3
    key_centre, key_near, key_far, key_rows = jax.random.split(key, 4)
    centre = jax.random.randint(key_centre, (FRAMES, 1), 0, tile_count)
    local_block = jnp.arange(BLOCKS).astype(jnp.int32) % BLK_DEV
    group = (local_block // CAP)[None, :]
    near_plane = centre * tile_width + jax.random.randint(key_near, (FRAMES, BLOCKS), 0, tile_width)
    region_first = (centre + centre_span + (group - 1) * region) * tile_width
    far_plane = region_first + jax.random.randint(key_far, (FRAMES, BLOCKS), 0, region * tile_width - 5)
    plane = jnp.where(group == 0, near_plane, far_plane) % GRID
    row_first = jax.random.randint(key_rows, (FRAMES, BLOCKS), 0, GRID)
    return jnp.stack([plane, row_first], axis=-1).astype(jnp.int32)


def set_ends(values, rng, smallest, high):
    index_at = [jax.random.randint(jax.random.fold_in(rng, axis), (), 0, length) for axis, length in enumerate(values.shape)]
    widest = values.shape.index(max(values.shape))
    next_to = index_at[:widest] + [(index_at[widest] + 1) % values.shape[widest]] + index_at[widest + 1:]
    return values.at[tuple(index_at)].set(smallest).at[tuple(next_to)].set(high)


def steps_of(own_key, shape, pieces, low, high):
    def one(axis_at, blocks):
        heights = jax.random.uniform(jax.random.fold_in(jax.random.fold_in(own_key, 6), axis_at), (blocks,), jnp.float32, low / len(pieces), high / len(pieces))
        return jnp.repeat(jnp.exp(heights), shape[axis_at] // blocks).reshape((-1,) + (1,) * (len(shape) - axis_at - 1))

    loudness = one(*pieces[0])
    for cut in pieces[1:]:
        loudness = loudness * one(*cut)
    return loudness


def normal_values(stream_key, shape, deviation, limit, shards=(), kind=jnp.bfloat16):
    level = steps_of(stream_key, shape, shards, -0.22, 0.18) if shards else 1.0
    entries = jax.random.normal(stream_key, shape, jnp.float32) * deviation * level
    return jnp.minimum(jnp.maximum(entries, -limit), limit).astype(kind)


def setup_inputs(seed: int = 0) -> dict:
    splits = jax.random.split(jax.random.key(seed), 9)
    kspace_samples = normal_values(splits[0], (FRAMES, BLOCKS, 2 * COILS, SAMP), 1.0, 6.0, ((0, 8), (1, 32)))
    density = jnp.clip(jnp.exp(math.log(8.0) - 2.306499 * jax.random.uniform(splits[1], (FRAMES, BLOCKS, SAMP), jnp.float32) ** steps_of(splits[1], (FRAMES, BLOCKS, SAMP), ((0, 8), (1, 32)), -0.2, 0.2)), 0.796875, 8.0).astype(jnp.bfloat16)
    sample_frac = jnp.clip(1.0 * jax.random.uniform(splits[2], (FRAMES, BLOCKS, 3, SAMP), jnp.float32) ** steps_of(splits[2], (FRAMES, BLOCKS, 3, SAMP), ((0, 8), (1, 32)), -0.2, 0.2), 0.0, 1.0).astype(jnp.bfloat16)
    row_offsets = set_ends(jax.random.randint(splits[3], (FRAMES, BLOCKS, SAMP), 0, WIN - 5), jax.random.fold_in(splits[3], 1), 0, (WIN - 5) - 1).astype(jnp.int32)
    depth_base = set_ends(jax.random.randint(splits[4], (FRAMES, BLOCKS, SAMP), 0, GRID), jax.random.fold_in(splits[4], 1), 0, GRID - 1).astype(jnp.int32)
    block_base = draw_block_base(jax.random.fold_in(splits[8], 71), 0)
    coil_maps = normal_values(splits[6], (COILS, 2, GRID, GRID, GRID), 0.25, 1.5, ((2, 32),))
    estimate = normal_values(splits[7], (FRAMES, 2, GRID, GRID, GRID), 1.0, 6.0, ((0, 8), (2, 32)), jnp.float32)
    return {"kspace_samples": kspace_samples, "density": density, "sample_frac": sample_frac, "row_offsets": row_offsets, "depth_base": depth_base, "block_base": block_base, "coil_maps": coil_maps, "estimate": estimate}


BETA = 13.9
EPS = 0.05
LAMBDA_TV = 0.3

def bessel_zero(argument):
    quarter = argument * argument / 4.0
    series_term = jnp.ones_like(argument)
    series_sum = jnp.ones_like(argument)
    for power in range(1, 40):
        series_term = series_term * quarter / float(power * power)
        series_sum = series_sum + series_term
    return series_sum

def kaiser(offset, fraction):
    distance = offset.astype(jnp.float32) - 2.0 - fraction
    inside = jnp.maximum(1.0 - distance / 3.0 * (distance / 3.0), 0.0)
    return bessel_zero(BETA * jnp.sqrt(inside)) / bessel_zero(jnp.full_like(distance, BETA))

def to_bfloat(values):
    return lax.optimization_barrier(values.astype(jnp.bfloat16)).astype(jnp.float32)

def inverse_pass(real_part, imag_part, axis_pos):
    field = lax.complex(real_part, imag_part)
    result = jnp.fft.ifft(field, axis=axis_pos) * GRID
    return (jnp.real(result), jnp.imag(result))

def reference(kspace_samples, density, sample_frac, row_offsets, depth_base, block_base, coil_maps, estimate):
    scale = 1.0 / (8.0 * math.sqrt(SAMPLES))
    offsets = jnp.arange(6).astype(jnp.int32)
    maps_real = jnp.moveaxis(coil_maps[:, 0].astype(jnp.float32), 0, -1)
    maps_imag = jnp.moveaxis(coil_maps[:, 1].astype(jnp.float32), 0, -1)

    def one_frame(inputs):
        samples, weights, fractions, row_shift, depth_start, block_start = inputs
        channels = samples.shape[1]
        frac_x = fractions[:, 0].astype(jnp.float32)
        frac_y = fractions[:, 1].astype(jnp.float32)
        frac_z = fractions[:, 2].astype(jnp.float32)
        along_x = kaiser(offsets[:, None, None], frac_x[None])
        along_y = kaiser(offsets[:, None, None], frac_y[None])
        along_z = to_bfloat(kaiser(offsets[:, None, None], frac_z[None]))
        amplitude = weights.astype(jnp.float32)[:, :, None] * jnp.swapaxes(samples, 1, 2).astype(jnp.float32)
        row_first = block_start[:, 1][:, None] + row_shift
        y_pos = (row_first[None] + offsets[:, None, None]) % GRID
        z_pos = (depth_start[None] + offsets[:, None, None]) % GRID
        cells = jnp.zeros((GRID * GRID * GRID, channels), jnp.float32)
        for tap_index in range(6):
            x_pos = (block_start[:, 0] + tap_index) % GRID
            outer = to_bfloat(amplitude[None] * along_x[tap_index][None, :, :, None] * along_y[:, :, :, None])
            values = outer[:, None] * along_z[None, :, :, :, None]
            flat = (y_pos[:, None] * GRID + x_pos[None, None, :, None]) * GRID + z_pos[None]
            cells = cells.at[flat.reshape(-1).astype(jnp.int32)].add(values.reshape(-1, channels))
        kspace = to_bfloat(cells).reshape(GRID, GRID, GRID, channels // 2, 2)
        real_part, imag_part = inverse_pass(kspace[..., 0], kspace[..., 1], 0)
        real_part, imag_part = (to_bfloat(real_part), to_bfloat(imag_part))
        real_part, imag_part = inverse_pass(real_part, imag_part, 2)
        real_part, imag_part = (to_bfloat(real_part), to_bfloat(imag_part))
        real_part, imag_part = inverse_pass(real_part, imag_part, 1)
        back_real = scale * lax.optimization_barrier(jnp.sum(maps_real * real_part + maps_imag * imag_part, axis=-1))
        back_imag = scale * lax.optimization_barrier(jnp.sum(maps_real * imag_part - maps_imag * real_part, axis=-1))
        return jnp.stack([back_real, back_imag], axis=0)
    back = lax.map(one_frame, (kspace_samples, density, sample_frac, row_offsets, depth_base, block_base))
    half = estimate + back
    change = half[1:] - half[:-1]
    magnitude = jnp.sqrt(change[:, 0] * change[:, 0] + change[:, 1] * change[:, 1] + EPS * EPS)
    psi = change / magnitude[:, None]
    zero_frame = jnp.zeros_like(psi[:1])
    psi_before = jnp.concatenate([zero_frame, psi], axis=0)
    psi_after = jnp.concatenate([psi, zero_frame], axis=0)
    return half - LAMBDA_TV * (psi_before - psi_after)
```

```python
import functools
import math

import jax
import jax.numpy as jnp
import numpy as np
from jax import lax
from jax.experimental import pallas as pl
from jax.experimental.pallas import tpu as pltpu
from jax.sharding import PartitionSpec as P

MESH = pl.DeviceIdType.MESH
BETA = 13.9
EPS = 0.05
LAMBDA_TV = 0.3
TAPS = 6
POWERS = 40

ROW_WX, ROW_XB, ROW_WZ, ROW_WY, ROW_YB, ROW_ZB, ROWS = 32, 38, 40, 48, 54, 55, 56


def kaiser_coefficients():
    terms, term = [], 1.0
    for power in range(POWERS):
        if power:
            term *= BETA * BETA / 4.0 / (power * power)
        terms.append(term)
    total = sum(terms)
    return [term / total for term in terms]


def kaiser(offset, fraction):
    distance = (offset - 2.0 - fraction) * (1.0 / 3.0)
    inside = jnp.maximum(1.0 - distance * distance, 0.0)
    terms = kaiser_coefficients()
    result = jnp.full_like(inside, terms[-1])
    for term in reversed(terms[:-1]):
        result = result * inside + term
    return result


def dft_tables(size):
    index = np.arange(size)
    angles = (index[:, None] * index[None, :] % size) * (2.0 * np.pi / size)
    cosine, sine = np.cos(angles), np.sin(angles)
    right = np.block([[cosine, sine], [-sine, cosine]])
    left = np.block([[cosine, -sine], [sine, cosine]])
    return right.astype(np.float32), left.astype(np.float32)


def message_kernel(samples_ref, density_ref, frac_ref, shift_ref, depth_ref, base_ref, out_ref, lines_ref):
    frames, blocks, channels, lanes = samples_ref.shape
    coils = channels // 2
    grid_mask = 127
    row = lax.broadcasted_iota(jnp.int32, (8, lanes), 0)
    offset = row.astype(jnp.float32)
    for frame in range(frames):
        for block in range(blocks):
            slot = frame * blocks + block
            lines_ref[slot] = samples_ref[frame, block].astype(jnp.float32) * density_ref[frame, block : block + 1].astype(jnp.float32)
            taps = [
                jnp.where(row < TAPS, kaiser(offset, frac_ref[frame, block, axis : axis + 1].astype(jnp.float32)), 0.0)
                for axis in range(3)
            ]
            plane = base_ref[frame, block, 0].astype(jnp.float32)
            first_row = (shift_ref[frame, block : block + 1] + base_ref[frame, block, 1]) & grid_mask
            first_cell = depth_ref[frame, block : block + 1]
            group_x = jnp.where(row == ROW_XB - ROW_WX, plane, taps[0])
            group_y = jnp.where(row == ROW_YB - ROW_WY, first_row.astype(jnp.float32), taps[1])
            group_y = jnp.where(row == ROW_ZB - ROW_WY, first_cell.astype(jnp.float32), group_y)
            out_ref[frame, block, 0:coils] = lines_ref[slot, pl.ds(0, coils, stride=2), :].astype(jnp.bfloat16)
            out_ref[frame, block, coils:channels] = lines_ref[slot, pl.ds(1, coils, stride=2), :].astype(jnp.bfloat16)
            out_ref[frame, block, ROW_WX : ROW_WX + 16] = jnp.concatenate([group_x, taps[2]], axis=0).astype(jnp.bfloat16)
            out_ref[frame, block, ROW_WY : ROW_WY + 8] = group_y.astype(jnp.bfloat16)


def row_tables(image_rows, grid, lanes):
    angle_of = lambda index: (index % grid).astype(jnp.float32) * (2.0 * math.pi / grid)
    turn = angle_of(image_rows[:, None] * jnp.arange(lanes)[None, :])
    step = jnp.broadcast_to(angle_of(jnp.arange(TAPS)[:, None] * image_rows[None, :])[:, :, None], (TAPS, image_rows.shape[0], lanes))
    angles = jnp.concatenate([turn[None], step], axis=0)
    cosine, sine = jnp.cos(angles), jnp.sin(angles)
    rows = lambda upper, lower: jnp.concatenate([upper, lower], axis=1)
    return jnp.concatenate(
        [rows(cosine, sine)[:1], rows(sine, cosine)[:1], rows(cosine, cosine)[1:], rows(-sine, sine)[1:]], axis=0
    )


def block_messages(kspace_samples, density, sample_frac, row_offsets, depth_base, block_base):
    frames, blocks, channels, lanes = kspace_samples.shape
    vmem, smem = pl.BlockSpec(memory_space=pltpu.VMEM), pl.BlockSpec(memory_space=pltpu.SMEM)
    return pl.pallas_call(
        message_kernel,
        out_shape=jax.ShapeDtypeStruct((frames, blocks, ROWS, lanes), jnp.bfloat16),
        in_specs=[vmem] * 5 + [smem],
        out_specs=vmem,
        scratch_shapes=[pltpu.VMEM((frames * blocks, channels, lanes), jnp.float32)],
        name="message",
    )(kspace_samples, density, sample_frac, row_offsets, depth_base, block_base)


def gather_kernel(side, msg_ref, out_ref, send_sem, recv_sem, own_sem):
    tile = lax.axis_index("tile")
    core, chip = tile % 2, tile // 2
    chip_x, chip_y = chip // side, chip % side
    first = chip_x + core * (chip_y - chip_x)
    other = chip_y + core * (chip_x - chip_y)
    first_step = 2 * side - (2 * side - 2) * core
    other_step = 2 + (2 * side - 2) * core

    def at(along, across):
        return ((first + along + side) % side) * first_step + ((other + across + side) % side) * other_step + core

    partner = tile + 1 - 2 * core
    neighbours = [at(1, 0), at(-1, 0), at(0, 1), at(0, -1), partner]

    barrier = pltpu.get_barrier_semaphore()
    for device in neighbours:
        pl.semaphore_signal(barrier, inc=1, device_id={"tile": device}, device_id_type=MESH)
    pl.semaphore_wait(barrier, len(neighbours))

    def whole(number, slot, target, own=False):
        return pltpu.make_async_remote_copy(
            src_ref=msg_ref if own else out_ref.at[slot],
            dst_ref=out_ref.at[slot],
            send_sem=send_sem.at[number],
            recv_sem=recv_sem.at[number],
            device_id={"tile": target},
            device_id_type=MESH,
        )

    def part(number, slot, frame, target):
        return pltpu.make_async_remote_copy(
            src_ref=out_ref.at[slot, frame],
            dst_ref=out_ref.at[slot, frame],
            send_sem=send_sem.at[number],
            recv_sem=recv_sem.at[number],
            device_id={"tile": target},
            device_id_type=MESH,
        )

    copies = {0: whole(0, tile, at(1, 0), True), 1: whole(1, tile, at(-1, 0), True)}
    copies[2] = part(2, at(-1, 0), 0, at(1, 0))
    copies[3] = part(3, at(1, 0), 1, at(-1, 0))
    places = [0, -1, 1, 2]
    for index, along in enumerate(places):
        base = 4 + 4 * index
        copies[base] = whole(base, at(along, 0), at(0, 1), along == 0)
        copies[base + 1] = whole(base + 1, at(along, 0), at(0, -1), along == 0)
        copies[base + 2] = part(base + 2, at(along, -1), 0, at(0, 1))
        copies[base + 3] = part(base + 3, at(along, 1), 1, at(0, -1))
        for turn, across in enumerate(places):
            number = 20 + 4 * index + turn
            copies[number] = whole(number, at(along, across), partner, along == 0 and across == 0)

    def start(*numbers):
        for number in numbers:
            copies[number].start()

    def arrived(*numbers):
        for number in numbers:
            copies[number].wait_recv()

    own = pltpu.make_async_copy(msg_ref, out_ref.at[tile], own_sem)
    start(0, 1, 4, 5, 20)
    own.start()
    arrived(0)
    start(2, 8, 9, 24)
    arrived(1)
    start(3, 12, 13, 28)
    arrived(4)
    start(6, 21)
    arrived(5)
    start(7, 22)
    arrived(2, 3)
    start(16, 17, 32)
    for index in (1, 2, 3):
        base = 4 + 4 * index
        arrived(base)
        start(base + 2, 20 + 4 * index + 1)
        arrived(base + 1)
        start(base + 3, 20 + 4 * index + 2)
    for index in range(4):
        base = 4 + 4 * index
        arrived(base + 2, base + 3)
        start(20 + 4 * index + 3)
    arrived(*range(20, 36))
    for number in range(36):
        copies[number].wait_send()
    own.wait()


def gather_messages(message, tiles, side):
    return pl.pallas_call(
        functools.partial(gather_kernel, side),
        out_shape=jax.ShapeDtypeStruct((tiles,) + message.shape, message.dtype),
        in_specs=[pl.BlockSpec(memory_space=pltpu.VMEM)],
        out_specs=pl.BlockSpec(memory_space=pl.ANY),
        scratch_shapes=[
            pltpu.SemaphoreType.DMA((36,)),
            pltpu.SemaphoreType.DMA((36,)),
            pltpu.SemaphoreType.DMA(()),
        ],
        compiler_params=pltpu.CompilerParams(collective_id=0, has_side_effects=True),
        name="gather",
    )(message)


def grid_kernel(grid, coils, rows, blocks, scale, xb_ref, msg_ref, tables_ref, right_ref, left_ref, maps_ref, est_ref, out_ref, acc_ref):
    frame = pl.program_id(0)
    half_rows = rows * coils
    plane = 2 * half_rows
    per_tile = msg_ref.shape[2]

    def clear(step, carry):
        acc_ref[pl.ds(pl.multiple_of(step * 128, 128), 128), :] = jnp.zeros((128, grid), jnp.float32)
        return carry

    lax.fori_loop(0, grid * plane // 128, clear, 0, unroll=4)
    cells = lax.broadcasted_iota(jnp.int32, (8, 128), 0)

    def one_block(block, carry):
        tile, local = block // per_tile, block % per_tile
        real = msg_ref[tile, 0, local, 0:coils, :].astype(jnp.float32)
        imag = msg_ref[tile, 0, local, coils : 2 * coils, :].astype(jnp.float32)
        weights = msg_ref[tile, 0, local, ROW_WX : ROW_WX + 8, :].astype(jnp.float32)
        depth = msg_ref[tile, 0, local, ROW_WZ : ROW_WZ + 8, :].astype(jnp.float32)
        tail = msg_ref[tile, 0, local, ROW_WY : ROW_WY + 8, :].astype(jnp.float32)
        first_row = jnp.broadcast_to(tail[ROW_YB - ROW_WY : ROW_YB - ROW_WY + 1, :].astype(jnp.int32), (8, 128))
        first_cell = tail[ROW_ZB - ROW_WY : ROW_ZB - ROW_WY + 1, :].astype(jnp.int32)
        turn = jnp.take_along_axis(tables_ref[0], first_row, axis=1)
        swapped = jnp.take_along_axis(tables_ref[1], first_row, axis=1)
        sum_same = sum(tail[e : e + 1] * tables_ref[2 + e] for e in range(TAPS))
        sum_cross = sum(tail[e : e + 1] * tables_ref[2 + TAPS + e] for e in range(TAPS))
        phase = turn * sum_same + swapped * sum_cross
        reals = [real * phase[y : y + 1] - imag * phase[rows + y : rows + y + 1] for y in range(rows)]
        imags = [real * phase[rows + y : rows + y + 1] + imag * phase[y : y + 1] for y in range(rows)]
        field = jnp.concatenate(reals + imags, axis=0)
        lag0 = cells - first_cell
        pieces = []
        for group in range(grid // 8):
            lag = jnp.minimum((lag0 + group * 8) & (grid - 1), 7)
            pieces.append(jnp.take_along_axis(depth, lag, axis=0))
        spread = jnp.concatenate(pieces, axis=0).astype(jnp.bfloat16)
        left = jnp.concatenate([(field * weights[tap : tap + 1]).astype(jnp.bfloat16) for tap in range(TAPS)], axis=0)
        value = lax.dot_general(left, spread, (((1,), (1,)), ((), ())), preferred_element_type=jnp.float32)
        first_plane = xb_ref[frame, block]
        for tap in range(TAPS):
            start = pl.multiple_of(((first_plane + tap) & (grid - 1)) * plane, plane)
            acc_ref[pl.ds(start, plane), :] += value[tap * plane : (tap + 1) * plane]
        return carry

    lax.fori_loop(0, blocks, one_block, 0, unroll=4)

    right = right_ref[...]
    left = left_ref[...]
    for y in range(rows):
        out_ref[0, 0, y] = jnp.zeros((grid, grid), jnp.float32)
        out_ref[0, 1, y] = jnp.zeros((grid, grid), jnp.float32)

        def one_pair(pair, carry, y=y):
            coil = pair * 2
            lines = []
            for part in range(2):
                base = y * coils + coil + part
                re = acc_ref[pl.ds(base, grid, stride=plane), :]
                im = acc_ref[pl.ds(half_rows + base, grid, stride=plane), :]
                lines.append(jnp.concatenate([re, im], axis=1).astype(jnp.bfloat16))
            second = jnp.dot(jnp.concatenate(lines, axis=0), right, preferred_element_type=jnp.float32).astype(jnp.bfloat16)
            stacked = jnp.concatenate(
                [
                    jnp.concatenate([second[:grid, :grid], second[grid:, :grid]], axis=1),
                    jnp.concatenate([second[:grid, grid:], second[grid:, grid:]], axis=1),
                ],
                axis=0,
            )
            image = jnp.dot(left, stacked, preferred_element_type=jnp.float32)
            back_re = jnp.zeros((grid, grid), jnp.float32)
            back_im = jnp.zeros((grid, grid), jnp.float32)
            for part in range(2):
                image_re = image[:grid, part * grid : (part + 1) * grid]
                image_im = image[grid:, part * grid : (part + 1) * grid]
                map_re = maps_ref[coil + part, 0, y].astype(jnp.float32)
                map_im = maps_ref[coil + part, 1, y].astype(jnp.float32)
                back_re += map_re * image_re + map_im * image_im
                back_im += map_re * image_im - map_im * image_re
            out_ref[0, 0, y] += back_re
            out_ref[0, 1, y] += back_im
            return carry

        lax.fori_loop(0, coils // 2, one_pair, 0, unroll=8)
        out_ref[0, 0, y] = est_ref[0, 0, y] + scale * out_ref[0, 0, y]
        out_ref[0, 1, y] = est_ref[0, 1, y] + scale * out_ref[0, 1, y]


def half_step(gathered, first_plane, tables, coil_maps, estimate, scale):
    tiles, frames, per_tile = gathered.shape[:3]
    coils, _, rows, grid, _ = coil_maps.shape
    blocks = tiles * per_tile
    right, left = (jnp.asarray(table, jnp.bfloat16) for table in dft_tables(grid))
    once = pl.Buffered(1)
    return pl.pallas_call(
        functools.partial(grid_kernel, grid, coils, rows, blocks, scale),
        out_shape=jax.ShapeDtypeStruct(estimate.shape, jnp.float32),
        grid_spec=pltpu.PrefetchScalarGridSpec(
            num_scalar_prefetch=1,
            grid=(frames,),
            in_specs=[
                pl.BlockSpec((tiles, 1, per_tile, ROWS, 128), lambda f, s: (0, f, 0, 0, 0)),
                pl.BlockSpec(tables.shape, lambda f, s: (0, 0, 0), pipeline_mode=once),
                pl.BlockSpec((2 * grid, 2 * grid), lambda f, s: (0, 0), pipeline_mode=once),
                pl.BlockSpec((2 * grid, 2 * grid), lambda f, s: (0, 0), pipeline_mode=once),
                pl.BlockSpec(coil_maps.shape, lambda f, s: (0, 0, 0, 0, 0), pipeline_mode=once),
                pl.BlockSpec((1, 2, rows, grid, grid), lambda f, s: (f, 0, 0, 0, 0)),
            ],
            out_specs=pl.BlockSpec((1, 2, rows, grid, grid), lambda f, s: (f, 0, 0, 0, 0)),
            scratch_shapes=[pltpu.VMEM((grid * 2 * rows * coils, grid), jnp.float32)],
        ),
        compiler_params=pltpu.CompilerParams(vmem_limit_bytes=56 * 1024 * 1024),
        name="grid",
    )(first_plane, gathered, tables, right, left, coil_maps, estimate)


def on_device(
    kspace_samples, density, sample_frac, row_offsets, depth_base, block_base, coil_maps, estimate
):
    tile_count = lax.axis_size("tile")
    tile_here = lax.axis_index("tile")
    frame_here = lax.axis_index("frame")
    frames, per_tile, channels, samples = kspace_samples.shape
    coils = channels // 2
    grid = coil_maps.shape[3]
    rows = coil_maps.shape[2]
    scale = 1.0 / (8.0 * math.sqrt(per_tile * tile_count * samples))

    message = block_messages(kspace_samples, density, sample_frac, row_offsets, depth_base, block_base)
    gathered = gather_messages(message, tile_count, math.isqrt(tile_count // 2))

    first_plane = gathered[:, :, :, ROW_XB, 0].astype(jnp.int32)
    first_plane = jnp.moveaxis(first_plane, 1, 0).reshape(frames, tile_count * per_tile)
    tables = row_tables(tile_here * rows + jnp.arange(rows), grid, samples)
    half = half_step(gathered, first_plane, tables, coil_maps, estimate, scale)

    count = lax.axis_size("frame")
    forward = [(i, i + 1) for i in range(count - 1)]
    backward = [(target, source) for source, target in forward]
    low = lax.ppermute(half[-1:].astype(jnp.bfloat16), "frame", forward)
    high = lax.ppermute(half[:1].astype(jnp.bfloat16), "frame", backward)
    padded = jnp.concatenate([low.astype(jnp.float32), half, high.astype(jnp.float32)], axis=0)
    change = padded[1:] - padded[:-1]
    magnitude = jnp.sqrt(change[:, 0] * change[:, 0] + change[:, 1] * change[:, 1] + EPS * EPS)
    psi = change / magnitude[:, None]
    pair_index = frame_here * frames + jnp.arange(frames + 1) - 1
    valid = (pair_index >= 0) & (pair_index <= count * frames - 2)
    psi = jnp.where(valid[:, None, None, None, None], psi, 0.0)
    return half - LAMBDA_TV * (psi[:-1] - psi[1:])


def solution(mesh):
    in_specs = (
        P("frame", "tile", None, None),
        P("frame", "tile", None),
        P("frame", "tile", None, None),
        P("frame", "tile", None),
        P("frame", "tile", None),
        P("frame", "tile", None),
        P(None, None, "tile", None, None),
        P("frame", None, "tile", None, None),
    )
    out_specs = P("frame", None, "tile", None, None)
    return jax.shard_map(
        on_device, mesh=mesh, in_specs=in_specs, out_specs=out_specs, check_vma=False
    )
```

```python
import functools
import math

import jax
import jax.numpy as jnp
import numpy as np
from jax import lax
from jax.experimental import pallas as pl
from jax.experimental.pallas import tpu as pltpu
from jax.sharding import PartitionSpec as P

MESH = pl.DeviceIdType.MESH
BETA = 13.9
EPS = 0.05
LAMBDA_TV = 0.3
TAPS = 6
POWERS = 40

ROW_WX, ROW_XB, ROW_WZ, ROW_WY, ROW_YB, ROW_ZB, ROWS = 32, 38, 40, 48, 54, 55, 56


def kaiser_coefficients():
    terms, term = [], 1.0
    for power in range(POWERS):
        if power:
            term *= BETA * BETA / 4.0 / (power * power)
        terms.append(term)
    total = sum(terms)
    return [term / total for term in terms]


def kaiser(offset, fraction):
    distance = (offset - 2.0 - fraction) * (1.0 / 3.0)
    inside = jnp.maximum(1.0 - distance * distance, 0.0)
    terms = kaiser_coefficients()
    result = jnp.full_like(inside, terms[-1])
    for term in reversed(terms[:-1]):
        result = result * inside + term
    return result


def dft_tables(size):
    index = np.arange(size)
    angles = (index[:, None] * index[None, :] % size) * (2.0 * np.pi / size)
    cosine, sine = np.cos(angles), np.sin(angles)
    right = np.block([[cosine, sine], [-sine, cosine]])
    left = np.block([[cosine, -sine], [sine, cosine]])
    return right.astype(np.float32), left.astype(np.float32)


def message_kernel(samples_ref, density_ref, frac_ref, shift_ref, depth_ref, base_ref, out_ref, lines_ref):
    frames, blocks, channels, lanes = samples_ref.shape
    coils = channels // 2
    grid_mask = 127
    row = lax.broadcasted_iota(jnp.int32, (8, lanes), 0)
    offset = row.astype(jnp.float32)
    for frame in range(frames):
        for block in range(blocks):
            slot = frame * blocks + block
            lines_ref[slot] = samples_ref[frame, block].astype(jnp.float32) * density_ref[frame, block : block + 1].astype(jnp.float32)
            taps = [
                jnp.where(row < TAPS, kaiser(offset, frac_ref[frame, axis, block : block + 1].astype(jnp.float32)), 0.0)
                for axis in range(3)
            ]
            plane = base_ref[frame, 0, block].astype(jnp.float32)
            first_row = (shift_ref[frame, block : block + 1] + base_ref[frame, 1, block]) & grid_mask
            first_cell = depth_ref[frame, block : block + 1]
            group_x = jnp.where(row == ROW_XB - ROW_WX, plane, taps[0])
            group_y = jnp.where(row == ROW_YB - ROW_WY, first_row.astype(jnp.float32), taps[1])
            group_y = jnp.where(row == ROW_ZB - ROW_WY, first_cell.astype(jnp.float32), group_y)
            out_ref[frame, block, 0:coils] = lines_ref[slot, pl.ds(0, coils, stride=2), :].astype(jnp.bfloat16)
            out_ref[frame, block, coils:channels] = lines_ref[slot, pl.ds(1, coils, stride=2), :].astype(jnp.bfloat16)
            out_ref[frame, block, ROW_WX : ROW_WX + 16] = jnp.concatenate([group_x, taps[2]], axis=0).astype(jnp.bfloat16)
            out_ref[frame, block, ROW_WY : ROW_WY + 8] = group_y.astype(jnp.bfloat16)


def row_tables(rows, grid, lanes):
    image_rows = np.arange(grid).reshape(grid // rows, rows, 1)
    angles = (image_rows * np.arange(lanes) % grid) * (2.0 * np.pi / grid)
    cosine, sine = np.cos(angles), np.sin(angles)
    pairs = [(cosine, sine), (sine, cosine), (cosine, cosine), (-sine, sine)]
    return np.stack([np.concatenate(pair, axis=1) for pair in pairs], axis=1).astype(np.float32)


def block_messages(kspace_samples, density, sample_frac, row_offsets, depth_base, block_base):
    frames, blocks, channels, lanes = kspace_samples.shape
    vmem, smem = pl.BlockSpec(memory_space=pltpu.VMEM), pl.BlockSpec(memory_space=pltpu.SMEM)
    return pl.pallas_call(
        message_kernel,
        out_shape=jax.ShapeDtypeStruct((frames, blocks, ROWS, lanes), jnp.bfloat16),
        in_specs=[vmem] * 5 + [smem],
        out_specs=vmem,
        scratch_shapes=[pltpu.VMEM((frames * blocks, channels, lanes), jnp.float32)],
        name="message",
    )(kspace_samples, density, jnp.swapaxes(sample_frac, 1, 2), row_offsets, depth_base, jnp.swapaxes(block_base, 1, 2))


def gather_kernel(side, msg_ref, out_ref, send_sem, recv_sem, own_sem):
    tile = lax.axis_index("tile")
    core, chip = tile % 2, tile // 2
    chip_x, chip_y = chip // side, chip % side
    first = chip_x + core * (chip_y - chip_x)
    other = chip_y + core * (chip_x - chip_y)
    first_step = 2 * side - (2 * side - 2) * core
    other_step = 2 + (2 * side - 2) * core

    def at(along, across):
        return ((first + along + side) % side) * first_step + ((other + across + side) % side) * other_step + core

    partner = tile + 1 - 2 * core
    neighbours = [at(1, 0), at(-1, 0), at(0, 1), at(0, -1), partner]

    barrier = pltpu.get_barrier_semaphore()
    for device in neighbours:
        pl.semaphore_signal(barrier, inc=1, device_id={"tile": device}, device_id_type=MESH)
    pl.semaphore_wait(barrier, len(neighbours))

    def whole(number, slot, target, own=False):
        return pltpu.make_async_remote_copy(
            src_ref=msg_ref if own else out_ref.at[slot],
            dst_ref=out_ref.at[slot],
            send_sem=send_sem.at[number],
            recv_sem=recv_sem.at[number],
            device_id={"tile": target},
            device_id_type=MESH,
        )

    def part(number, slot, frame, target):
        return pltpu.make_async_remote_copy(
            src_ref=out_ref.at[slot, frame],
            dst_ref=out_ref.at[slot, frame],
            send_sem=send_sem.at[number],
            recv_sem=recv_sem.at[number],
            device_id={"tile": target},
            device_id_type=MESH,
        )

    copies = {0: whole(0, tile, at(1, 0), True), 1: whole(1, tile, at(-1, 0), True)}
    copies[2] = part(2, at(-1, 0), 0, at(1, 0))
    copies[3] = part(3, at(1, 0), 1, at(-1, 0))
    places = [0, -1, 1, 2]
    for index, along in enumerate(places):
        base = 4 + 4 * index
        copies[base] = whole(base, at(along, 0), at(0, 1), along == 0)
        copies[base + 1] = whole(base + 1, at(along, 0), at(0, -1), along == 0)
        copies[base + 2] = part(base + 2, at(along, -1), 0, at(0, 1))
        copies[base + 3] = part(base + 3, at(along, 1), 1, at(0, -1))
        for turn, across in enumerate(places):
            number = 20 + 4 * index + turn
            copies[number] = whole(number, at(along, across), partner, along == 0 and across == 0)

    def start(*numbers):
        for number in numbers:
            copies[number].start()

    def arrived(*numbers):
        for number in numbers:
            copies[number].wait_recv()

    own = pltpu.make_async_copy(msg_ref, out_ref.at[tile], own_sem)
    start(0, 1, 4, 5, 20)
    own.start()
    arrived(0)
    start(2, 8, 9, 24)
    arrived(1)
    start(3, 12, 13, 28)
    arrived(4)
    start(6, 21)
    arrived(5)
    start(7, 22)
    arrived(2, 3)
    start(16, 17, 32)
    for index in (1, 2, 3):
        base = 4 + 4 * index
        arrived(base)
        start(base + 2, 20 + 4 * index + 1)
        arrived(base + 1)
        start(base + 3, 20 + 4 * index + 2)
    for index in range(4):
        base = 4 + 4 * index
        arrived(base + 2, base + 3)
        start(20 + 4 * index + 3)
    arrived(*range(20, 36))
    for number in range(36):
        copies[number].wait_send()
    own.wait()


def gather_messages(message, tiles, side):
    return pl.pallas_call(
        functools.partial(gather_kernel, side),
        out_shape=jax.ShapeDtypeStruct((tiles,) + message.shape, message.dtype),
        in_specs=[pl.BlockSpec(memory_space=pltpu.VMEM)],
        out_specs=pl.BlockSpec(memory_space=pl.ANY),
        scratch_shapes=[
            pltpu.SemaphoreType.DMA((36,)),
            pltpu.SemaphoreType.DMA((36,)),
            pltpu.SemaphoreType.DMA(()),
        ],
        compiler_params=pltpu.CompilerParams(collective_id=0, has_side_effects=True),
        name="gather",
    )(message)


def grid_kernel(grid, coils, rows, blocks, scale, tile_ref, msg_ref, tables_ref, right_ref, left_ref, maps_ref, est_ref, out_ref, acc_ref, steps_ref):
    here = tile_ref[0]
    half_rows = rows * coils
    plane = 2 * half_rows
    per_tile = msg_ref.shape[2]
    pitch = plane + 8

    def clear(step, carry):
        acc_ref[pl.ds(pl.multiple_of(step * 128, 128), 128), :] = jnp.zeros((128, grid), jnp.float32)
        return carry

    lax.fori_loop(0, grid * pitch // 128, clear, 0, unroll=4)
    for tap in range(TAPS):
        steps_ref[tap] = jnp.broadcast_to(tables_ref[here, 2][:, tap : tap + 1], (2 * rows, 128))
        steps_ref[TAPS + tap] = jnp.broadcast_to(tables_ref[here, 3][:, tap : tap + 1], (2 * rows, 128))
    cells = lax.broadcasted_iota(jnp.int32, (8, 128), 0)

    def one_block(block, carry):
        tile, local = block // per_tile, block % per_tile
        real = msg_ref[tile, 0, local, 0:coils, :].astype(jnp.float32)
        imag = msg_ref[tile, 0, local, coils : 2 * coils, :].astype(jnp.float32)
        weights = msg_ref[tile, 0, local, ROW_WX : ROW_WX + 8, :].astype(jnp.float32)
        depth = msg_ref[tile, 0, local, ROW_WZ : ROW_WZ + 8, :].astype(jnp.float32)
        tail = msg_ref[tile, 0, local, ROW_WY : ROW_WY + 8, :].astype(jnp.float32)
        first_row = jnp.broadcast_to(tail[ROW_YB - ROW_WY : ROW_YB - ROW_WY + 1, :].astype(jnp.int32), (8, 128))
        first_cell = tail[ROW_ZB - ROW_WY : ROW_ZB - ROW_WY + 1, :].astype(jnp.int32)
        turn = jnp.take_along_axis(tables_ref[here, 0], first_row, axis=1)
        swapped = jnp.take_along_axis(tables_ref[here, 1], first_row, axis=1)
        sum_same = sum(tail[e : e + 1] * steps_ref[e] for e in range(TAPS))
        sum_cross = sum(tail[e : e + 1] * steps_ref[TAPS + e] for e in range(TAPS))
        phase = turn * sum_same + swapped * sum_cross
        reals = [real * phase[y : y + 1] - imag * phase[rows + y : rows + y + 1] for y in range(rows)]
        imags = [real * phase[rows + y : rows + y + 1] + imag * phase[y : y + 1] for y in range(rows)]
        field = jnp.concatenate(reals + imags, axis=0)
        low = cells - (first_cell & 15)
        inside = [jnp.take_along_axis(depth, jnp.minimum((low + part) & 31, 7), axis=0) for part in (0, 8)]
        after = [jnp.take_along_axis(depth, jnp.minimum(low + part, 7), axis=0) for part in (16, 24)]
        inside = jnp.concatenate(inside, axis=0).astype(jnp.bfloat16)
        after = jnp.concatenate(after, axis=0).astype(jnp.bfloat16)
        group = jnp.broadcast_to((first_cell >> 4).astype(jnp.float32), (16, 128)).astype(jnp.bfloat16)
        hits = [group == jnp.asarray(index, jnp.bfloat16) for index in range(grid // 16)]
        nothing = jnp.zeros((16, 128), jnp.bfloat16)
        spread = jnp.concatenate(
            [jnp.where(hits[index], inside, jnp.where(hits[index - 1], after, nothing)) for index in range(grid // 16)], axis=0
        )
        field16 = field.astype(jnp.bfloat16).reshape(plane // 16, 16, 128)
        left = jnp.concatenate(
            [field16 * jnp.broadcast_to(weights[tap : tap + 1], (16, 128)).astype(jnp.bfloat16)[None] for tap in range(TAPS)], axis=0
        ).reshape(TAPS * plane, 128)
        value = lax.dot_general(left, spread, (((1,), (1,)), ((), ())), preferred_element_type=jnp.float32)
        first_plane = weights[ROW_XB - ROW_WX : ROW_XB - ROW_WX + 1, :].astype(jnp.int32)[0, 0]
        for tap in range(TAPS):
            start = pl.multiple_of(((first_plane + tap) & (grid - 1)) * pitch, 8)
            acc_ref[pl.ds(start, plane), :] += value[tap * plane : (tap + 1) * plane]
        return carry

    lax.fori_loop(0, blocks, one_block, 0, unroll=32)

    right = right_ref[...]
    left = left_ref[...]
    for y in range(rows):
        out_ref[0, 0, y] = jnp.zeros((grid, grid), jnp.float32)
        out_ref[0, 1, y] = jnp.zeros((grid, grid), jnp.float32)

        def one_pair(pair, carry, y=y):
            coil = pair * 2
            lines = []
            for part in range(2):
                base = y * coils + coil + part
                re = acc_ref[pl.ds(base, grid, stride=pitch), :]
                im = acc_ref[pl.ds(half_rows + base, grid, stride=pitch), :]
                lines.append(jnp.concatenate([re, im], axis=1).astype(jnp.bfloat16))
            second = jnp.dot(jnp.concatenate(lines, axis=0), right, preferred_element_type=jnp.float32).astype(jnp.bfloat16)
            stacked = jnp.concatenate(
                [
                    jnp.concatenate([second[:grid, :grid], second[grid:, :grid]], axis=1),
                    jnp.concatenate([second[:grid, grid:], second[grid:, grid:]], axis=1),
                ],
                axis=0,
            )
            image = jnp.dot(left, stacked, preferred_element_type=jnp.float32)
            back_re = jnp.zeros((grid, grid), jnp.float32)
            back_im = jnp.zeros((grid, grid), jnp.float32)
            for part in range(2):
                image_re = image[:grid, part * grid : (part + 1) * grid]
                image_im = image[grid:, part * grid : (part + 1) * grid]
                map_re = maps_ref[coil + part, 0, y].astype(jnp.float32)
                map_im = maps_ref[coil + part, 1, y].astype(jnp.float32)
                back_re += map_re * image_re + map_im * image_im
                back_im += map_re * image_im - map_im * image_re
            out_ref[0, 0, y] += back_re
            out_ref[0, 1, y] += back_im
            return carry

        lax.fori_loop(0, coils // 2, one_pair, 0, unroll=8)
        out_ref[0, 0, y] = est_ref[0, 0, y] + scale * out_ref[0, 0, y]
        out_ref[0, 1, y] = est_ref[0, 1, y] + scale * out_ref[0, 1, y]


def half_step(gathered, tile, coil_maps, estimate, scale):
    tiles, frames, per_tile = gathered.shape[:3]
    coils, _, rows, grid, _ = coil_maps.shape
    blocks = tiles * per_tile
    right, left = (jnp.asarray(table, jnp.bfloat16) for table in dft_tables(grid))
    tables = jnp.asarray(row_tables(rows, grid, gathered.shape[-1]))
    once = pl.Buffered(1)
    return pl.pallas_call(
        functools.partial(grid_kernel, grid, coils, rows, blocks, scale),
        out_shape=jax.ShapeDtypeStruct(estimate.shape, jnp.float32),
        grid_spec=pltpu.PrefetchScalarGridSpec(
            num_scalar_prefetch=1,
            grid=(frames,),
            in_specs=[
                pl.BlockSpec((tiles, 1, per_tile, ROWS, 128), lambda f, s: (0, f, 0, 0, 0)),
                pl.BlockSpec(tables.shape, lambda f, s: (0, 0, 0, 0), pipeline_mode=once),
                pl.BlockSpec((2 * grid, 2 * grid), lambda f, s: (0, 0), pipeline_mode=once),
                pl.BlockSpec((2 * grid, 2 * grid), lambda f, s: (0, 0), pipeline_mode=once),
                pl.BlockSpec(coil_maps.shape, lambda f, s: (0, 0, 0, 0, 0), pipeline_mode=once),
                pl.BlockSpec((1, 2, rows, grid, grid), lambda f, s: (f, 0, 0, 0, 0)),
            ],
            out_specs=pl.BlockSpec((1, 2, rows, grid, grid), lambda f, s: (f, 0, 0, 0, 0)),
            scratch_shapes=[
                pltpu.VMEM((grid * (2 * rows * coils + 8), grid), jnp.float32),
                pltpu.VMEM((2 * TAPS, 2 * rows, 128), jnp.float32),
            ],
        ),
        compiler_params=pltpu.CompilerParams(vmem_limit_bytes=56 * 1024 * 1024),
        name="grid",
    )(tile, gathered, tables, right, left, coil_maps, estimate)


def on_device(
    kspace_samples, density, sample_frac, row_offsets, depth_base, block_base, coil_maps, estimate
):
    tile_count = lax.axis_size("tile")
    tile_here = lax.axis_index("tile")
    frame_here = lax.axis_index("frame")
    frames, per_tile, channels, samples = kspace_samples.shape
    coils = channels // 2
    grid = coil_maps.shape[3]
    rows = coil_maps.shape[2]
    scale = 1.0 / (8.0 * math.sqrt(per_tile * tile_count * samples))

    message = block_messages(kspace_samples, density, sample_frac, row_offsets, depth_base, block_base)
    gathered = gather_messages(message, tile_count, math.isqrt(tile_count // 2))

    half = half_step(gathered, tile_here.reshape(1), coil_maps, estimate, scale)

    count = lax.axis_size("frame")
    forward = [(i, i + 1) for i in range(count - 1)]
    backward = [(target, source) for source, target in forward]
    low = lax.ppermute(half[-1:].astype(jnp.bfloat16), "frame", forward)
    high = lax.ppermute(half[:1].astype(jnp.bfloat16), "frame", backward)
    padded = jnp.concatenate([low.astype(jnp.float32), half, high.astype(jnp.float32)], axis=0)
    change = padded[1:] - padded[:-1]
    magnitude = jnp.sqrt(change[:, 0] * change[:, 0] + change[:, 1] * change[:, 1] + EPS * EPS)
    psi = change / magnitude[:, None]
    pair_index = frame_here * frames + jnp.arange(frames + 1) - 1
    valid = (pair_index >= 0) & (pair_index <= count * frames - 2)
    psi = jnp.where(valid[:, None, None, None, None], psi, 0.0)
    return half - LAMBDA_TV * (psi[:-1] - psi[1:])


def solution(mesh):
    in_specs = (
        P("frame", "tile", None, None),
        P("frame", "tile", None),
        P("frame", "tile", None, None),
        P("frame", "tile", None),
        P("frame", "tile", None),
        P("frame", "tile", None),
        P(None, None, "tile", None, None),
        P("frame", None, "tile", None, None),
    )
    out_specs = P("frame", None, "tile", None, None)
    return jax.shard_map(
        on_device, mesh=mesh, in_specs=in_specs, out_specs=out_specs, check_vma=False
    )
```

```python
import functools
import math

import jax
import jax.numpy as jnp
import numpy as np
from jax import lax
from jax.experimental import pallas as pl
from jax.experimental.pallas import tpu as pltpu
from jax.sharding import PartitionSpec as P

MESH = pl.DeviceIdType.MESH
BETA = 13.9
EPS = 0.05
LAMBDA_TV = 0.3
TAPS = 6
POWERS = 40

ROW_WX, ROW_XB, ROW_WZ, ROW_WY, ROW_YB, ROW_ZB, ROWS = 32, 38, 40, 48, 54, 55, 56


def kaiser_coefficients():
    terms, term = [], 1.0
    for power in range(POWERS):
        if power:
            term *= BETA * BETA / 4.0 / (power * power)
        terms.append(term)
    total = sum(terms)
    return [term / total for term in terms]


def kaiser(offset, fraction):
    distance = (offset - 2.0 - fraction) * (1.0 / 3.0)
    inside = jnp.maximum(1.0 - distance * distance, 0.0)
    terms = kaiser_coefficients()
    result = jnp.full_like(inside, terms[-1])
    for term in reversed(terms[:-1]):
        result = result * inside + term
    return result


def dft_tables(size):
    index = np.arange(size)
    angles = (index[:, None] * index[None, :] % size) * (2.0 * np.pi / size)
    cosine, sine = np.cos(angles), np.sin(angles)
    right = np.block([[cosine, sine], [-sine, cosine]])
    left = np.block([[cosine, -sine], [sine, cosine]])
    return right.astype(np.float32), left.astype(np.float32)


def message_kernel(samples_ref, density_ref, frac_ref, shift_ref, depth_ref, base_ref, out_ref, lines_ref):
    frames, blocks, channels, lanes = samples_ref.shape
    coils = channels // 2
    grid_mask = 127
    row = lax.broadcasted_iota(jnp.int32, (8, lanes), 0)
    offset = row.astype(jnp.float32)
    for frame in range(frames):
        for block in range(blocks):
            slot = frame * blocks + block
            lines_ref[slot] = samples_ref[frame, block].astype(jnp.float32) * density_ref[frame, block : block + 1].astype(jnp.float32)
            taps = [
                jnp.where(row < TAPS, kaiser(offset, frac_ref[frame, axis, block : block + 1].astype(jnp.float32)), 0.0)
                for axis in range(3)
            ]
            plane = base_ref[frame, 0, block].astype(jnp.float32)
            first_row = (shift_ref[frame, block : block + 1] + base_ref[frame, 1, block]) & grid_mask
            first_cell = depth_ref[frame, block : block + 1]
            group_x = jnp.where(row == ROW_XB - ROW_WX, plane, taps[0])
            group_y = jnp.where(row == ROW_YB - ROW_WY, first_row.astype(jnp.float32), taps[1])
            group_y = jnp.where(row == ROW_ZB - ROW_WY, first_cell.astype(jnp.float32), group_y)
            out_ref[frame, block, 0:coils] = lines_ref[slot, pl.ds(0, coils, stride=2), :].astype(jnp.bfloat16)
            out_ref[frame, block, coils:channels] = lines_ref[slot, pl.ds(1, coils, stride=2), :].astype(jnp.bfloat16)
            out_ref[frame, block, ROW_WX : ROW_WX + 16] = jnp.concatenate([group_x, taps[2]], axis=0).astype(jnp.bfloat16)
            out_ref[frame, block, ROW_WY : ROW_WY + 8] = group_y.astype(jnp.bfloat16)


def row_tables(rows, grid, lanes):
    image_rows = np.arange(grid).reshape(grid // rows, rows, 1)
    angles = (image_rows * np.arange(lanes) % grid) * (2.0 * np.pi / grid)
    cosine, sine = np.cos(angles), np.sin(angles)
    pairs = [(cosine, sine), (sine, cosine), (cosine, cosine), (-sine, sine)]
    return np.stack([np.concatenate(pair, axis=1) for pair in pairs], axis=1).astype(np.float32)


def block_messages(kspace_samples, density, sample_frac, row_offsets, depth_base, block_base):
    frames, blocks, channels, lanes = kspace_samples.shape
    vmem, smem = pl.BlockSpec(memory_space=pltpu.VMEM), pl.BlockSpec(memory_space=pltpu.SMEM)
    return pl.pallas_call(
        message_kernel,
        out_shape=jax.ShapeDtypeStruct((frames, blocks, ROWS, lanes), jnp.bfloat16),
        in_specs=[vmem] * 5 + [smem],
        out_specs=vmem,
        scratch_shapes=[pltpu.VMEM((frames * blocks, channels, lanes), jnp.float32)],
        name="message",
    )(kspace_samples, density, jnp.swapaxes(sample_frac, 1, 2), row_offsets, depth_base, jnp.swapaxes(block_base, 1, 2))


def gather_kernel(side, msg_ref, out_ref, send_sem, recv_sem, own_sem):
    tile = lax.axis_index("tile")
    core, chip = tile % 2, tile // 2
    chip_x, chip_y = chip // side, chip % side
    first = chip_x + core * (chip_y - chip_x)
    other = chip_y + core * (chip_x - chip_y)
    first_step = 2 * side - (2 * side - 2) * core
    other_step = 2 + (2 * side - 2) * core

    def at(along, across):
        return ((first + along + side) % side) * first_step + ((other + across + side) % side) * other_step + core

    partner = tile + 1 - 2 * core
    neighbours = [at(1, 0), at(-1, 0), at(0, 1), at(0, -1), partner]

    barrier = pltpu.get_barrier_semaphore()
    for device in neighbours:
        pl.semaphore_signal(barrier, inc=1, device_id={"tile": device}, device_id_type=MESH)
    pl.semaphore_wait(barrier, len(neighbours))

    copies = {}

    def make(key, slot, frame, target, own):
        number = len(copies)
        source = msg_ref if own else out_ref.at[slot]
        copies[key] = pltpu.make_async_remote_copy(
            src_ref=source if frame is None else source.at[frame],
            dst_ref=out_ref.at[slot] if frame is None else out_ref.at[slot, frame],
            send_sem=send_sem.at[number],
            recv_sem=recv_sem.at[number],
            device_id={"tile": target},
            device_id_type=MESH,
        )

    for frame in (0, 1):
        for way in (1, -1):
            make(("first", 0, frame, way), tile, frame, at(way, 0), True)
    make(("pass", 0), at(-1, 0), 0, at(1, 0), False)
    make(("pass", 1), at(1, 0), 1, at(-1, 0), False)
    for along in (0, -1, 1, 2):
        for frame in (0, 1):
            for way in (1, -1):
                make(("second", along, frame, way), at(along, 0), frame, at(0, way), along == 0)
        make(("hand", along, 0), at(along, -1), 0, at(0, 1), False)
        make(("hand", along, 1), at(along, 1), 1, at(0, -1), False)
        for across in (0, -1, 1, 2):
            make(("core", along, across), at(along, across), None, partner, along == 0 and across == 0)

    def start(*keys):
        for key in keys:
            copies[key].start()

    def arrived(*keys):
        for key in keys:
            copies[key].wait_recv()

    def second(along, *frames):
        for frame in frames:
            way = 1 - 2 * frame
            start(("second", along, frame, way), ("second", along, frame, -way))

    there = {}

    def to_core(along, across, *frames):
        there[along, across] = there.get((along, across), 0) + len(frames)
        if there[along, across] == 2:
            start(("core", along, across))

    own = pltpu.make_async_copy(msg_ref, out_ref.at[tile], own_sem)
    start(("first", 0, 0, 1), ("first", 0, 1, -1), ("first", 0, 1, 1), ("first", 0, 0, -1))
    second(0, 0, 1)
    own.start()
    to_core(0, 0, 0, 1)
    arrived(("first", 0, 0, 1))
    start(("pass", 0))
    second(-1, 0)
    to_core(-1, 0, 0)
    arrived(("first", 0, 1, -1))
    start(("pass", 1))
    second(1, 1)
    to_core(1, 0, 1)
    arrived(("first", 0, 1, 1))
    second(-1, 1)
    to_core(-1, 0, 1)
    arrived(("first", 0, 0, -1))
    second(1, 0)
    to_core(1, 0, 0)
    arrived(("second", 0, 0, 1))
    start(("hand", 0, 0))
    to_core(0, -1, 0)
    arrived(("second", 0, 1, -1))
    start(("hand", 0, 1))
    to_core(0, 1, 1)
    arrived(("pass", 0))
    second(2, 0)
    to_core(2, 0, 0)
    arrived(("pass", 1))
    second(2, 1)
    to_core(2, 0, 1)
    arrived(("second", 0, 1, 1))
    to_core(0, -1, 1)
    arrived(("second", 0, 0, -1))
    to_core(0, 1, 0)
    for along in (-1, 1, 2):
        order = (0, 1) if along != 1 else (1, 0)
        for frame in order:
            way = 1 - 2 * frame
            arrived(("second", along, frame, way))
            start(("hand", along, frame))
            to_core(along, -way, frame)
        for frame in order:
            way = 1 - 2 * frame
            arrived(("second", along, frame, -way))
            to_core(along, way, frame)
    for along in (0, -1, 1, 2):
        for frame in (0, 1):
            arrived(("hand", along, frame))
            to_core(along, 2, frame)
    for key in [key for key in copies if key[0] == "core"]:
        copies[key].wait_recv()
    for copy in copies.values():
        copy.wait_send()
    own.wait()


def gather_messages(message, tiles, side):
    return pl.pallas_call(
        functools.partial(gather_kernel, side),
        out_shape=jax.ShapeDtypeStruct((tiles,) + message.shape, message.dtype),
        in_specs=[pl.BlockSpec(memory_space=pltpu.VMEM)],
        out_specs=pl.BlockSpec(memory_space=pl.ANY),
        scratch_shapes=[
            pltpu.SemaphoreType.DMA((46,)),
            pltpu.SemaphoreType.DMA((46,)),
            pltpu.SemaphoreType.DMA(()),
        ],
        compiler_params=pltpu.CompilerParams(collective_id=0, has_side_effects=True),
        name="gather",
    )(message)


def grid_kernel(grid, coils, rows, blocks, scale, tile_ref, msg_ref, tables_ref, right_ref, left_ref, maps_ref, est_ref, out_ref, sent_ref, acc_ref, steps_ref):
    here = tile_ref[0]
    half_rows = rows * coils
    plane = 2 * half_rows
    per_tile = msg_ref.shape[2]
    pitch = plane + 8

    def clear(step, carry):
        acc_ref[pl.ds(pl.multiple_of(step * 128, 128), 128), :] = jnp.zeros((128, grid), jnp.float32)
        return carry

    lax.fori_loop(0, grid * pitch // 128, clear, 0, unroll=4)
    for tap in range(TAPS):
        steps_ref[tap] = jnp.broadcast_to(tables_ref[here, 2][:, tap : tap + 1], (2 * rows, 128))
        steps_ref[TAPS + tap] = jnp.broadcast_to(tables_ref[here, 3][:, tap : tap + 1], (2 * rows, 128))
    cells = lax.broadcasted_iota(jnp.int32, (8, 128), 0)

    def one_block(block, carry):
        tile, local = block // per_tile, block % per_tile
        real = msg_ref[tile, 0, local, 0:coils, :].astype(jnp.float32)
        imag = msg_ref[tile, 0, local, coils : 2 * coils, :].astype(jnp.float32)
        weights = msg_ref[tile, 0, local, ROW_WX : ROW_WX + 8, :].astype(jnp.float32)
        depth = msg_ref[tile, 0, local, ROW_WZ : ROW_WZ + 8, :].astype(jnp.float32)
        tail = msg_ref[tile, 0, local, ROW_WY : ROW_WY + 8, :].astype(jnp.float32)
        first_row = jnp.broadcast_to(tail[ROW_YB - ROW_WY : ROW_YB - ROW_WY + 1, :].astype(jnp.int32), (8, 128))
        first_cell = tail[ROW_ZB - ROW_WY : ROW_ZB - ROW_WY + 1, :].astype(jnp.int32)
        turn = jnp.take_along_axis(tables_ref[here, 0], first_row, axis=1)
        swapped = jnp.take_along_axis(tables_ref[here, 1], first_row, axis=1)
        sum_same = sum(tail[e : e + 1] * steps_ref[e] for e in range(TAPS))
        sum_cross = sum(tail[e : e + 1] * steps_ref[TAPS + e] for e in range(TAPS))
        phase = turn * sum_same + swapped * sum_cross
        reals = [real * phase[y : y + 1] - imag * phase[rows + y : rows + y + 1] for y in range(rows)]
        imags = [real * phase[rows + y : rows + y + 1] + imag * phase[y : y + 1] for y in range(rows)]
        field = jnp.concatenate(reals + imags, axis=0)
        low = cells - (first_cell & 15)
        inside = [jnp.take_along_axis(depth, jnp.minimum((low + part) & 31, 7), axis=0) for part in (0, 8)]
        after = [jnp.take_along_axis(depth, jnp.minimum(low + part, 7), axis=0) for part in (16, 24)]
        inside = jnp.concatenate(inside, axis=0).astype(jnp.bfloat16)
        after = jnp.concatenate(after, axis=0).astype(jnp.bfloat16)
        group = jnp.broadcast_to((first_cell >> 4).astype(jnp.float32), (16, 128)).astype(jnp.bfloat16)
        hits = [group == jnp.asarray(index, jnp.bfloat16) for index in range(grid // 16)]
        nothing = jnp.zeros((16, 128), jnp.bfloat16)
        spread = jnp.concatenate(
            [jnp.where(hits[index], inside, jnp.where(hits[index - 1], after, nothing)) for index in range(grid // 16)], axis=0
        )
        field16 = field.astype(jnp.bfloat16).reshape(plane // 16, 16, 128)
        left = jnp.concatenate(
            [field16 * jnp.broadcast_to(weights[tap : tap + 1], (16, 128)).astype(jnp.bfloat16)[None] for tap in range(TAPS)], axis=0
        ).reshape(TAPS * plane, 128)
        value = lax.dot_general(left, spread, (((1,), (1,)), ((), ())), preferred_element_type=jnp.float32)
        first_plane = weights[ROW_XB - ROW_WX : ROW_XB - ROW_WX + 1, :].astype(jnp.int32)[0, 0]
        for tap in range(TAPS):
            start = pl.multiple_of(((first_plane + tap) & (grid - 1)) * pitch, 8)
            acc_ref[pl.ds(start, plane), :] += value[tap * plane : (tap + 1) * plane]
        return carry

    lax.fori_loop(0, blocks, one_block, 0, unroll=32)

    right = right_ref[...]
    left = left_ref[...]
    for y in range(rows):
        out_ref[0, 0, y] = jnp.zeros((grid, grid), jnp.float32)
        out_ref[0, 1, y] = jnp.zeros((grid, grid), jnp.float32)

        def one_pair(pair, carry, y=y):
            coil = pair * 2
            lines = []
            for part in range(2):
                base = y * coils + coil + part
                re = acc_ref[pl.ds(base, grid, stride=pitch), :]
                im = acc_ref[pl.ds(half_rows + base, grid, stride=pitch), :]
                lines.append(jnp.concatenate([re, im], axis=1).astype(jnp.bfloat16))
            second = jnp.dot(jnp.concatenate(lines, axis=0), right, preferred_element_type=jnp.float32).astype(jnp.bfloat16)
            stacked = jnp.concatenate(
                [
                    jnp.concatenate([second[:grid, :grid], second[grid:, :grid]], axis=1),
                    jnp.concatenate([second[:grid, grid:], second[grid:, grid:]], axis=1),
                ],
                axis=0,
            )
            image = jnp.dot(left, stacked, preferred_element_type=jnp.float32)
            back_re = jnp.zeros((grid, grid), jnp.float32)
            back_im = jnp.zeros((grid, grid), jnp.float32)
            for part in range(2):
                image_re = image[:grid, part * grid : (part + 1) * grid]
                image_im = image[grid:, part * grid : (part + 1) * grid]
                map_re = maps_ref[coil + part, 0, y].astype(jnp.float32)
                map_im = maps_ref[coil + part, 1, y].astype(jnp.float32)
                back_re += map_re * image_re + map_im * image_im
                back_im += map_re * image_im - map_im * image_re
            out_ref[0, 0, y] += back_re
            out_ref[0, 1, y] += back_im
            return carry

        lax.fori_loop(0, coils // 2, one_pair, 0, unroll=8)
        for part in range(2):
            half = est_ref[0, part, y] + scale * out_ref[0, part, y]
            out_ref[0, part, y] = half
            sent_ref[0, part, y] = half.astype(jnp.bfloat16)


def half_step(gathered, tile, coil_maps, estimate, scale):
    tiles, frames, per_tile = gathered.shape[:3]
    coils, _, rows, grid, _ = coil_maps.shape
    blocks = tiles * per_tile
    right, left = (jnp.asarray(table, jnp.bfloat16) for table in dft_tables(grid))
    tables = jnp.asarray(row_tables(rows, grid, gathered.shape[-1]))
    once = pl.Buffered(1)
    return pl.pallas_call(
        functools.partial(grid_kernel, grid, coils, rows, blocks, scale),
        out_shape=[jax.ShapeDtypeStruct(estimate.shape, kind) for kind in (jnp.float32, jnp.bfloat16)],
        grid_spec=pltpu.PrefetchScalarGridSpec(
            num_scalar_prefetch=1,
            grid=(frames,),
            in_specs=[
                pl.BlockSpec((tiles, 1, per_tile, ROWS, 128), lambda f, s: (0, f, 0, 0, 0)),
                pl.BlockSpec(tables.shape, lambda f, s: (0, 0, 0, 0), pipeline_mode=once),
                pl.BlockSpec((2 * grid, 2 * grid), lambda f, s: (0, 0), pipeline_mode=once),
                pl.BlockSpec((2 * grid, 2 * grid), lambda f, s: (0, 0), pipeline_mode=once),
                pl.BlockSpec(coil_maps.shape, lambda f, s: (0, 0, 0, 0, 0), pipeline_mode=once),
                pl.BlockSpec((1, 2, rows, grid, grid), lambda f, s: (f, 0, 0, 0, 0)),
            ],
            out_specs=[pl.BlockSpec((1, 2, rows, grid, grid), lambda f, s: (f, 0, 0, 0, 0))] * 2,
            scratch_shapes=[
                pltpu.VMEM((grid * (2 * rows * coils + 8), grid), jnp.float32),
                pltpu.VMEM((2 * TAPS, 2 * rows, 128), jnp.float32),
            ],
        ),
        compiler_params=pltpu.CompilerParams(vmem_limit_bytes=56 * 1024 * 1024),
        name="grid",
    )(tile, gathered, tables, right, left, coil_maps, estimate)


def exchange_kernel(count, half_ref, before_ref, after_ref, send_sem, recv_sem):
    here = lax.axis_index("frame")
    upper, lower = (here + 1) % count, (here + count - 1) % count
    barrier = pltpu.get_barrier_semaphore()
    for device in (upper, lower):
        pl.semaphore_signal(barrier, inc=1, device_id={"frame": device}, device_id_type=MESH)
    pl.semaphore_wait(barrier, 2)
    copies = [
        pltpu.make_async_remote_copy(
            src_ref=half_ref.at[frame],
            dst_ref=target,
            send_sem=send_sem.at[number],
            recv_sem=recv_sem.at[number],
            device_id={"frame": device},
            device_id_type=MESH,
        )
        for number, (frame, target, device) in enumerate(
            [(half_ref.shape[0] - 1, before_ref, upper), (0, after_ref, lower)]
        )
    ]
    for copy in copies:
        copy.start()
    for copy in copies:
        copy.wait()


def exchange_frames(half, count):
    anywhere = pl.BlockSpec(memory_space=pl.ANY)
    return pl.pallas_call(
        functools.partial(exchange_kernel, count),
        out_shape=[jax.ShapeDtypeStruct(half.shape[1:], half.dtype)] * 2,
        in_specs=[anywhere],
        out_specs=[anywhere] * 2,
        scratch_shapes=[pltpu.SemaphoreType.DMA((2,)), pltpu.SemaphoreType.DMA((2,))],
        compiler_params=pltpu.CompilerParams(collective_id=1, has_side_effects=True),
        name="exchange",
    )(half)


def variation_kernel(count, frame_ref, half_ref, before_ref, after_ref, out_ref):
    here = frame_ref[0]

    def psi(later, earlier):
        change = [later[part] - earlier[part] for part in range(2)]
        factor = lax.rsqrt(change[0] * change[0] + change[1] * change[1] + EPS * EPS)
        return [change[part] * factor for part in range(2)]

    first = [half_ref[0, part, 0] for part in range(2)]
    last = [half_ref[1, part, 0] for part in range(2)]
    before = [before_ref[part, 0].astype(jnp.float32) for part in range(2)]
    after = [after_ref[part, 0].astype(jnp.float32) for part in range(2)]
    psi_before, psi_here, psi_after = psi(first, before), psi(last, first), psi(after, last)
    for part in range(2):
        low = jnp.where(here > 0, psi_before[part], 0.0)
        high = jnp.where(here < count - 1, psi_after[part], 0.0)
        out_ref[0, part, 0] = first[part] - LAMBDA_TV * (low - psi_here[part])
        out_ref[1, part, 0] = last[part] - LAMBDA_TV * (psi_here[part] - high)


def variation_step(half, before, after, frame_here, count):
    frames, parts, rows, grid, _ = half.shape
    assert frames == 2
    whole = pl.BlockSpec((frames, parts, 1, grid, grid), lambda y, s: (0, 0, y, 0, 0))
    side = pl.BlockSpec((parts, 1, grid, grid), lambda y, s: (0, y, 0, 0))
    return pl.pallas_call(
        functools.partial(variation_kernel, count),
        out_shape=jax.ShapeDtypeStruct(half.shape, half.dtype),
        grid_spec=pltpu.PrefetchScalarGridSpec(
            num_scalar_prefetch=1, grid=(rows,), in_specs=[whole, side, side], out_specs=whole
        ),
        name="variation",
    )(frame_here, half, before, after)


def on_device(
    kspace_samples, density, sample_frac, row_offsets, depth_base, block_base, coil_maps, estimate
):
    tile_count = lax.axis_size("tile")
    tile_here = lax.axis_index("tile")
    frame_here = lax.axis_index("frame")
    frames, per_tile, channels, samples = kspace_samples.shape
    coils = channels // 2
    grid = coil_maps.shape[3]
    rows = coil_maps.shape[2]
    scale = 1.0 / (8.0 * math.sqrt(per_tile * tile_count * samples))

    message = block_messages(kspace_samples, density, sample_frac, row_offsets, depth_base, block_base)
    gathered = gather_messages(message, tile_count, math.isqrt(tile_count // 2))

    half, rounded = half_step(gathered, tile_here.reshape(1), coil_maps, estimate, scale)
    before, after = exchange_frames(rounded, lax.axis_size("frame"))
    return variation_step(half, before, after, frame_here.reshape(1), lax.axis_size("frame"))


def solution(mesh):
    in_specs = (
        P("frame", "tile", None, None),
        P("frame", "tile", None),
        P("frame", "tile", None, None),
        P("frame", "tile", None),
        P("frame", "tile", None),
        P("frame", "tile", None),
        P(None, None, "tile", None, None),
        P("frame", None, "tile", None, None),
    )
    out_specs = P("frame", None, "tile", None, None)
    return jax.shard_map(
        on_device, mesh=mesh, in_specs=in_specs, out_specs=out_specs, check_vma=False
    )
```

```python
import functools
import math

import jax
import jax.numpy as jnp
import numpy as np
from jax import lax
from jax.experimental import pallas as pl
from jax.experimental.pallas import tpu as pltpu
from jax.sharding import PartitionSpec as P

MESH = pl.DeviceIdType.MESH
BETA = 13.9
EPS = 0.05
LAMBDA_TV = 0.3
TAPS = 6
POWERS = 40

ROW_WX, ROW_XB, ROW_WZ, ROW_WY, ROW_YB, ROW_ZB, ROWS = 32, 38, 40, 48, 54, 55, 56


def kaiser_coefficients():
    terms, term = [], 1.0
    for power in range(POWERS):
        if power:
            term *= BETA * BETA / 4.0 / (power * power)
        terms.append(term)
    total = sum(terms)
    return [term / total for term in terms]


def kaiser(offset, fraction):
    distance = (offset - 2.0 - fraction) * (1.0 / 3.0)
    inside = jnp.maximum(1.0 - distance * distance, 0.0)
    terms = kaiser_coefficients()
    result = jnp.full_like(inside, terms[-1])
    for term in reversed(terms[:-1]):
        result = result * inside + term
    return result


def dft_tables(size):
    index = np.arange(size)
    angles = (index[:, None] * index[None, :] % size) * (2.0 * np.pi / size)
    cosine, sine = np.cos(angles), np.sin(angles)
    right = np.block([[cosine, sine], [-sine, cosine]])
    left = np.block([[cosine, -sine], [sine, cosine]])
    return right.astype(np.float32), left.astype(np.float32)


def write_message(samples_ref, density_ref, frac_ref, shift_ref, depth_ref, base_ref, out_ref, lines_ref):
    frames, blocks, channels, lanes = samples_ref.shape
    coils = channels // 2
    grid_mask = 127
    row = lax.broadcasted_iota(jnp.int32, (8, lanes), 0)
    offset = row.astype(jnp.float32)
    for frame in range(frames):
        for block in range(blocks):
            slot = frame * blocks + block
            lines_ref[slot] = samples_ref[frame, block].astype(jnp.float32) * density_ref[frame, block : block + 1].astype(jnp.float32)
            taps = [
                jnp.where(row < TAPS, kaiser(offset, frac_ref[frame, axis, block : block + 1].astype(jnp.float32)), 0.0)
                for axis in range(3)
            ]
            plane = base_ref[frame, 0, block].astype(jnp.float32)
            first_row = (shift_ref[frame, block : block + 1] + base_ref[frame, 1, block]) & grid_mask
            first_cell = depth_ref[frame, block : block + 1]
            group_x = jnp.where(row == ROW_XB - ROW_WX, plane, taps[0])
            group_y = jnp.where(row == ROW_YB - ROW_WY, first_row.astype(jnp.float32), taps[1])
            group_y = jnp.where(row == ROW_ZB - ROW_WY, first_cell.astype(jnp.float32), group_y)
            out_ref[frame, block, 0:coils] = lines_ref[slot, pl.ds(0, coils, stride=2), :].astype(jnp.bfloat16)
            out_ref[frame, block, coils:channels] = lines_ref[slot, pl.ds(1, coils, stride=2), :].astype(jnp.bfloat16)
            out_ref[frame, block, ROW_WX : ROW_WX + 16] = jnp.concatenate([group_x, taps[2]], axis=0).astype(jnp.bfloat16)
            out_ref[frame, block, ROW_WY : ROW_WY + 8] = group_y.astype(jnp.bfloat16)


def row_tables(rows, grid, lanes):
    image_rows = np.arange(grid).reshape(grid // rows, rows, 1)
    angles = (image_rows * np.arange(lanes) % grid) * (2.0 * np.pi / grid)
    cosine, sine = np.cos(angles), np.sin(angles)
    pairs = [(cosine, sine), (sine, cosine), (cosine, cosine), (-sine, sine)]
    return np.stack([np.concatenate(pair, axis=1) for pair in pairs], axis=1).astype(np.float32)


def gather_kernel(side, *refs):
    *input_refs, out_ref, msg_ref, lines_ref, send_sem, recv_sem, own_sem = refs
    tile = lax.axis_index("tile")
    core, chip = tile % 2, tile // 2
    chip_x, chip_y = chip // side, chip % side
    first = chip_x + core * (chip_y - chip_x)
    other = chip_y + core * (chip_x - chip_y)
    first_step = 2 * side - (2 * side - 2) * core
    other_step = 2 + (2 * side - 2) * core

    def at(along, across):
        return ((first + along + side) % side) * first_step + ((other + across + side) % side) * other_step + core

    partner = tile + 1 - 2 * core
    neighbours = [at(1, 0), at(-1, 0), at(0, 1), at(0, -1), partner]

    barrier = pltpu.get_barrier_semaphore()
    for device in neighbours:
        pl.semaphore_signal(barrier, inc=1, device_id={"tile": device}, device_id_type=MESH)
    write_message(*input_refs, msg_ref, lines_ref)
    pl.semaphore_wait(barrier, len(neighbours))

    copies = {}

    def make(key, slot, frame, target, own):
        number = len(copies)
        source = msg_ref if own else out_ref.at[slot]
        copies[key] = pltpu.make_async_remote_copy(
            src_ref=source if frame is None else source.at[frame],
            dst_ref=out_ref.at[slot] if frame is None else out_ref.at[slot, frame],
            send_sem=send_sem.at[number],
            recv_sem=recv_sem.at[number],
            device_id={"tile": target},
            device_id_type=MESH,
        )

    for frame in (0, 1):
        for way in (1, -1):
            make(("first", 0, frame, way), tile, frame, at(way, 0), True)
    make(("pass", 0), at(-1, 0), 0, at(1, 0), False)
    make(("pass", 1), at(1, 0), 1, at(-1, 0), False)
    for along in (0, -1, 1, 2):
        for frame in (0, 1):
            for way in (1, -1):
                make(("second", along, frame, way), at(along, 0), frame, at(0, way), along == 0)
        make(("hand", along, 0), at(along, -1), 0, at(0, 1), False)
        make(("hand", along, 1), at(along, 1), 1, at(0, -1), False)
        for across in (0, -1, 1, 2):
            make(("core", along, across), at(along, across), None, partner, along == 0 and across == 0)

    def start(*keys):
        for key in keys:
            copies[key].start()

    def arrived(*keys):
        for key in keys:
            copies[key].wait_recv()

    def second(along, *frames):
        for frame in frames:
            way = 1 - 2 * frame
            start(("second", along, frame, way), ("second", along, frame, -way))

    there = {}

    def to_core(along, across, *frames):
        there[along, across] = there.get((along, across), 0) + len(frames)
        if there[along, across] == 2:
            start(("core", along, across))

    own = pltpu.make_async_copy(msg_ref, out_ref.at[tile], own_sem)
    start(("first", 0, 0, 1), ("first", 0, 1, -1), ("first", 0, 1, 1), ("first", 0, 0, -1))
    second(0, 0, 1)
    own.start()
    to_core(0, 0, 0, 1)
    arrived(("first", 0, 0, 1))
    start(("pass", 0))
    second(-1, 0)
    to_core(-1, 0, 0)
    arrived(("first", 0, 1, -1))
    start(("pass", 1))
    second(1, 1)
    to_core(1, 0, 1)
    arrived(("first", 0, 1, 1))
    second(-1, 1)
    to_core(-1, 0, 1)
    arrived(("first", 0, 0, -1))
    second(1, 0)
    to_core(1, 0, 0)
    arrived(("second", 0, 0, 1))
    start(("hand", 0, 0))
    to_core(0, -1, 0)
    arrived(("second", 0, 1, -1))
    start(("hand", 0, 1))
    to_core(0, 1, 1)
    arrived(("pass", 0))
    second(2, 0)
    to_core(2, 0, 0)
    arrived(("pass", 1))
    second(2, 1)
    to_core(2, 0, 1)
    arrived(("second", 0, 1, 1))
    to_core(0, -1, 1)
    arrived(("second", 0, 0, -1))
    to_core(0, 1, 0)
    for along in (-1, 1, 2):
        order = (0, 1) if along != 1 else (1, 0)
        for frame in order:
            way = 1 - 2 * frame
            arrived(("second", along, frame, way))
            start(("hand", along, frame))
            to_core(along, -way, frame)
        for frame in order:
            way = 1 - 2 * frame
            arrived(("second", along, frame, -way))
            to_core(along, way, frame)
    for along in (0, -1, 1, 2):
        for frame in (0, 1):
            arrived(("hand", along, frame))
            to_core(along, 2, frame)
    for key in [key for key in copies if key[0] == "core"]:
        copies[key].wait_recv()
    for copy in copies.values():
        copy.wait_send()
    own.wait()


def gather_messages(kspace_samples, density, sample_frac, row_offsets, depth_base, block_base, tiles):
    frames, blocks, channels, lanes = kspace_samples.shape
    message = (frames, blocks, ROWS, lanes)
    vmem, smem = pl.BlockSpec(memory_space=pltpu.VMEM), pl.BlockSpec(memory_space=pltpu.SMEM)
    return pl.pallas_call(
        functools.partial(gather_kernel, math.isqrt(tiles // 2)),
        out_shape=jax.ShapeDtypeStruct((tiles,) + message, jnp.bfloat16),
        in_specs=[vmem] * 5 + [smem],
        out_specs=pl.BlockSpec(memory_space=pl.ANY),
        scratch_shapes=[
            pltpu.VMEM(message, jnp.bfloat16),
            pltpu.VMEM((frames * blocks, channels, lanes), jnp.float32),
            pltpu.SemaphoreType.DMA((46,)),
            pltpu.SemaphoreType.DMA((46,)),
            pltpu.SemaphoreType.DMA(()),
        ],
        compiler_params=pltpu.CompilerParams(collective_id=0, has_side_effects=True),
        name="gather",
    )(kspace_samples, density, jnp.swapaxes(sample_frac, 1, 2), row_offsets, depth_base, jnp.swapaxes(block_base, 1, 2))


def grid_kernel(grid, coils, rows, blocks, scale, tile_ref, msg_hbm, tables_hbm, right_ref, left_ref, maps_hbm, est_hbm, out_ref, sent_ref, acc_ref, steps_ref, lines_ref, msg_ref, tables_ref, maps_ref, est_ref, msg_sem, tables_sem, maps_sem, est_sem):
    frame = pl.program_id(0)
    half_rows = rows * coils

    def message_copy(which):
        return pltpu.make_async_copy(msg_hbm.at[:, which], msg_ref.at[which], msg_sem.at[which])

    tables_copy = pltpu.make_async_copy(tables_hbm.at[tile_ref[0]], tables_ref, tables_sem)
    maps_copy = pltpu.make_async_copy(maps_hbm, maps_ref, maps_sem)
    est_copy = pltpu.make_async_copy(est_hbm, est_ref, est_sem)

    @pl.when(frame == 0)
    def _():
        tables_copy.start()
        for which in range(2):
            message_copy(which).start()
        maps_copy.start()
        est_copy.start()

    plane = 2 * half_rows
    per_tile = msg_ref.shape[2]
    pitch = plane + 8

    def clear(step, carry):
        acc_ref[pl.ds(pl.multiple_of(step * 128, 128), 128), :] = jnp.zeros((128, grid), jnp.float32)
        return carry

    lax.fori_loop(0, grid * pitch // 128, clear, 0, unroll=4)
    @pl.when(frame == 0)
    def _():
        tables_copy.wait()

    message_copy(frame).wait()
    for tap in range(TAPS):
        steps_ref[tap] = jnp.broadcast_to(tables_ref[2][:, tap : tap + 1], (2 * rows, 128))
        steps_ref[TAPS + tap] = jnp.broadcast_to(tables_ref[3][:, tap : tap + 1], (2 * rows, 128))
    cells = lax.broadcasted_iota(jnp.int32, (8, 128), 0)

    def one_block(block, carry):
        tile, local = block // per_tile, block % per_tile
        real = msg_ref[frame, tile, local, 0:coils, :].astype(jnp.float32)
        imag = msg_ref[frame, tile, local, coils : 2 * coils, :].astype(jnp.float32)
        weights = msg_ref[frame, tile, local, ROW_WX : ROW_WX + 8, :].astype(jnp.float32)
        depth = msg_ref[frame, tile, local, ROW_WZ : ROW_WZ + 8, :].astype(jnp.float32)
        tail = msg_ref[frame, tile, local, ROW_WY : ROW_WY + 8, :].astype(jnp.float32)
        first_row = jnp.broadcast_to(tail[ROW_YB - ROW_WY : ROW_YB - ROW_WY + 1, :].astype(jnp.int32), (8, 128))
        first_cell = tail[ROW_ZB - ROW_WY : ROW_ZB - ROW_WY + 1, :].astype(jnp.int32)
        turn = jnp.take_along_axis(tables_ref[0], first_row, axis=1)
        swapped = jnp.take_along_axis(tables_ref[1], first_row, axis=1)
        sum_same = sum(tail[e : e + 1] * steps_ref[e] for e in range(TAPS))
        sum_cross = sum(tail[e : e + 1] * steps_ref[TAPS + e] for e in range(TAPS))
        phase = turn * sum_same + swapped * sum_cross
        reals = [real * phase[y : y + 1] - imag * phase[rows + y : rows + y + 1] for y in range(rows)]
        imags = [real * phase[rows + y : rows + y + 1] + imag * phase[y : y + 1] for y in range(rows)]
        field = jnp.concatenate(reals + imags, axis=0)
        low = cells - (first_cell & 15)
        inside = [jnp.take_along_axis(depth, jnp.minimum((low + part) & 31, 7), axis=0) for part in (0, 8)]
        after = [jnp.take_along_axis(depth, jnp.minimum(low + part, 7), axis=0) for part in (16, 24)]
        inside = jnp.concatenate(inside, axis=0).astype(jnp.bfloat16)
        after = jnp.concatenate(after, axis=0).astype(jnp.bfloat16)
        group = jnp.broadcast_to((first_cell >> 4).astype(jnp.float32), (16, 128)).astype(jnp.bfloat16)
        hits = [group == jnp.asarray(index, jnp.bfloat16) for index in range(grid // 16)]
        nothing = jnp.zeros((16, 128), jnp.bfloat16)
        spread = jnp.concatenate(
            [jnp.where(hits[index], inside, jnp.where(hits[index - 1], after, nothing)) for index in range(grid // 16)], axis=0
        )
        field16 = field.astype(jnp.bfloat16).reshape(plane // 16, 16, 128)
        left = jnp.concatenate(
            [field16 * jnp.broadcast_to(weights[tap : tap + 1], (16, 128)).astype(jnp.bfloat16)[None] for tap in range(TAPS)], axis=0
        ).reshape(TAPS * plane, 128)
        value = lax.dot_general(left, spread, (((1,), (1,)), ((), ())), preferred_element_type=jnp.float32)
        first_plane = weights[ROW_XB - ROW_WX : ROW_XB - ROW_WX + 1, :].astype(jnp.int32)[0, 0]
        for tap in range(TAPS):
            start = pl.multiple_of(((first_plane + tap) & (grid - 1)) * pitch, 8)
            acc_ref[pl.ds(start, plane), :] += value[tap * plane : (tap + 1) * plane]
        return carry

    lax.fori_loop(0, blocks, one_block, 0, unroll=32)

    @pl.when(frame == 0)
    def _():
        maps_copy.wait()
        est_copy.wait()

    right = right_ref[...]
    left = left_ref[...]
    for y in range(rows):
        out_ref[0, 0, y] = jnp.zeros((grid, grid), jnp.float32)
        out_ref[0, 1, y] = jnp.zeros((grid, grid), jnp.float32)

        for group in range(0, coils, 4):
            lines = []
            for coil in range(group, group + 4):
                base = y * coils + coil
                re = acc_ref[pl.ds(base, grid, stride=pitch), :]
                im = acc_ref[pl.ds(half_rows + base, grid, stride=pitch), :]
                lines.append(jnp.concatenate([re, im], axis=1).astype(jnp.bfloat16))
            lines_ref[group * grid : (group + 4) * grid] = jnp.dot(
                jnp.concatenate(lines, axis=0), right, preferred_element_type=jnp.float32
            ).astype(jnp.bfloat16)

        def one_pair(pair, carry, y=y):
            coil = pair * 2
            first_line = pl.multiple_of(coil * grid, 2 * grid)
            one, two = lines_ref[pl.ds(first_line, grid)], lines_ref[pl.ds(first_line + grid, grid)]
            stacked = jnp.concatenate(
                [
                    jnp.concatenate([one[:, :grid], two[:, :grid]], axis=1),
                    jnp.concatenate([one[:, grid:], two[:, grid:]], axis=1),
                ],
                axis=0,
            )
            image = jnp.dot(left, stacked, preferred_element_type=jnp.float32)
            back_re = jnp.zeros((grid, grid), jnp.float32)
            back_im = jnp.zeros((grid, grid), jnp.float32)
            for part in range(2):
                image_re = image[:grid, part * grid : (part + 1) * grid]
                image_im = image[grid:, part * grid : (part + 1) * grid]
                map_re = maps_ref[coil + part, 0, y].astype(jnp.float32)
                map_im = maps_ref[coil + part, 1, y].astype(jnp.float32)
                back_re += map_re * image_re + map_im * image_im
                back_im += map_re * image_im - map_im * image_re
            out_ref[0, 0, y] += back_re
            out_ref[0, 1, y] += back_im
            return carry

        lax.fori_loop(0, coils // 2, one_pair, 0, unroll=8)
        for part in range(2):
            half = est_ref[frame, part, y] + scale * out_ref[0, part, y]
            out_ref[0, part, y] = half
            sent_ref[0, part, y] = half.astype(jnp.bfloat16)


def half_step(gathered, tile, coil_maps, estimate, scale):
    tiles, frames, per_tile = gathered.shape[:3]
    coils, _, rows, grid, _ = coil_maps.shape
    blocks = tiles * per_tile
    right, left = (jnp.asarray(table, jnp.bfloat16) for table in dft_tables(grid))
    tables = jnp.asarray(row_tables(rows, grid, gathered.shape[-1]))
    once, anywhere = pl.Buffered(1), pl.BlockSpec(memory_space=pl.ANY)
    return pl.pallas_call(
        functools.partial(grid_kernel, grid, coils, rows, blocks, scale),
        out_shape=[jax.ShapeDtypeStruct(estimate.shape, kind) for kind in (jnp.float32, jnp.bfloat16)],
        grid_spec=pltpu.PrefetchScalarGridSpec(
            num_scalar_prefetch=1,
            grid=(frames,),
            in_specs=[
                anywhere,
                anywhere,
                pl.BlockSpec((2 * grid, 2 * grid), lambda f, s: (0, 0), pipeline_mode=once),
                pl.BlockSpec((2 * grid, 2 * grid), lambda f, s: (0, 0), pipeline_mode=once),
                anywhere,
                anywhere,
            ],
            out_specs=[pl.BlockSpec((1, 2, rows, grid, grid), lambda f, s: (f, 0, 0, 0, 0))] * 2,
            scratch_shapes=[
                pltpu.VMEM((grid * (2 * rows * coils + 8), grid), jnp.float32),
                pltpu.VMEM((2 * TAPS, 2 * rows, 128), jnp.float32),
                pltpu.VMEM((coils * grid, 2 * grid), jnp.bfloat16),
                pltpu.VMEM((frames, tiles, per_tile, ROWS, 128), gathered.dtype),
                pltpu.VMEM(tables.shape[1:], tables.dtype),
                pltpu.VMEM(coil_maps.shape, coil_maps.dtype),
                pltpu.VMEM(estimate.shape, estimate.dtype),
                pltpu.SemaphoreType.DMA((frames,)),
                pltpu.SemaphoreType.DMA(()),
                pltpu.SemaphoreType.DMA(()),
                pltpu.SemaphoreType.DMA(()),
            ],
        ),
        compiler_params=pltpu.CompilerParams(vmem_limit_bytes=56 * 1024 * 1024),
        name="grid",
    )(tile, gathered, tables, right, left, coil_maps, estimate)


def exchange_kernel(count, half_ref, before_ref, after_ref, send_sem, recv_sem):
    here = lax.axis_index("frame")
    upper, lower = (here + 1) % count, (here + count - 1) % count
    barrier = pltpu.get_barrier_semaphore()
    for device in (upper, lower):
        pl.semaphore_signal(barrier, inc=1, device_id={"frame": device}, device_id_type=MESH)
    pl.semaphore_wait(barrier, 2)
    copies = [
        pltpu.make_async_remote_copy(
            src_ref=half_ref.at[frame],
            dst_ref=target,
            send_sem=send_sem.at[number],
            recv_sem=recv_sem.at[number],
            device_id={"frame": device},
            device_id_type=MESH,
        )
        for number, (frame, target, device) in enumerate(
            [(half_ref.shape[0] - 1, before_ref, upper), (0, after_ref, lower)]
        )
    ]
    for copy in copies:
        copy.start()
    for copy in copies:
        copy.wait()


def exchange_frames(half, count):
    anywhere = pl.BlockSpec(memory_space=pl.ANY)
    return pl.pallas_call(
        functools.partial(exchange_kernel, count),
        out_shape=[jax.ShapeDtypeStruct(half.shape[1:], half.dtype)] * 2,
        in_specs=[anywhere],
        out_specs=[anywhere] * 2,
        scratch_shapes=[pltpu.SemaphoreType.DMA((2,)), pltpu.SemaphoreType.DMA((2,))],
        compiler_params=pltpu.CompilerParams(collective_id=1, has_side_effects=True),
        name="exchange",
    )(half)


def variation_kernel(count, frame_ref, half_ref, before_ref, after_ref, out_ref):
    here = frame_ref[0]

    def psi(later, earlier):
        change = [later[part] - earlier[part] for part in range(2)]
        factor = lax.rsqrt(change[0] * change[0] + change[1] * change[1] + EPS * EPS)
        return [change[part] * factor for part in range(2)]

    for y in range(half_ref.shape[2]):
        first = [half_ref[0, part, y] for part in range(2)]
        last = [half_ref[1, part, y] for part in range(2)]
        before = [before_ref[part, y].astype(jnp.float32) for part in range(2)]
        after = [after_ref[part, y].astype(jnp.float32) for part in range(2)]
        psi_before, psi_here, psi_after = psi(first, before), psi(last, first), psi(after, last)
        for part in range(2):
            low = jnp.where(here > 0, psi_before[part], 0.0)
            high = jnp.where(here < count - 1, psi_after[part], 0.0)
            out_ref[0, part, y] = first[part] - LAMBDA_TV * (low - psi_here[part])
            out_ref[1, part, y] = last[part] - LAMBDA_TV * (psi_here[part] - high)


def variation_step(half, before, after, frame_here, count):
    frames, parts, rows, grid, _ = half.shape
    assert frames == 2
    whole = pl.BlockSpec((frames, parts, rows // 2, grid, grid), lambda y, s: (0, 0, y, 0, 0))
    side = pl.BlockSpec((parts, rows // 2, grid, grid), lambda y, s: (0, y, 0, 0))
    return pl.pallas_call(
        functools.partial(variation_kernel, count),
        out_shape=jax.ShapeDtypeStruct(half.shape, half.dtype),
        grid_spec=pltpu.PrefetchScalarGridSpec(
            num_scalar_prefetch=1, grid=(2,), in_specs=[whole, side, side], out_specs=whole
        ),
        name="variation",
    )(frame_here, half, before, after)


def on_device(
    kspace_samples, density, sample_frac, row_offsets, depth_base, block_base, coil_maps, estimate
):
    tile_count = lax.axis_size("tile")
    tile_here = lax.axis_index("tile")
    frame_here = lax.axis_index("frame")
    frames, per_tile, channels, samples = kspace_samples.shape
    coils = channels // 2
    grid = coil_maps.shape[3]
    rows = coil_maps.shape[2]
    scale = 1.0 / (8.0 * math.sqrt(per_tile * tile_count * samples))

    gathered = gather_messages(
        kspace_samples, density, sample_frac, row_offsets, depth_base, block_base, tile_count
    )
    half, rounded = half_step(gathered, tile_here.reshape(1), coil_maps, estimate, scale)
    before, after = exchange_frames(rounded, lax.axis_size("frame"))
    return variation_step(half, before, after, frame_here.reshape(1), lax.axis_size("frame"))


def solution(mesh):
    in_specs = (
        P("frame", "tile", None, None),
        P("frame", "tile", None),
        P("frame", "tile", None, None),
        P("frame", "tile", None),
        P("frame", "tile", None),
        P("frame", "tile", None),
        P(None, None, "tile", None, None),
        P("frame", None, "tile", None, None),
    )
    out_specs = P("frame", None, "tile", None, None)
    return jax.shard_map(
        on_device, mesh=mesh, in_specs=in_specs, out_specs=out_specs, check_vma=False
    )
```

```python
import functools
import math

import jax
import jax.numpy as jnp
import numpy as np
from jax import lax
from jax.experimental import pallas as pl
from jax.experimental.pallas import tpu as pltpu
from jax.sharding import PartitionSpec as P

MESH = pl.DeviceIdType.MESH
BETA = 13.9
EPS = 0.05
LAMBDA_TV = 0.3
TAPS = 6
POWERS = 40

ROW_WX, ROW_XB, ROW_WZ, ROW_WY, ROW_YB, ROW_ZB, ROWS = 32, 38, 40, 48, 54, 55, 56


def kaiser_coefficients():
    terms, term = [], 1.0
    for power in range(POWERS):
        if power:
            term *= BETA * BETA / 4.0 / (power * power)
        terms.append(term)
    total = sum(terms)
    return [term / total for term in terms]


def kaiser(offset, fraction):
    distance = (offset - 2.0 - fraction) * (1.0 / 3.0)
    inside = jnp.maximum(1.0 - distance * distance, 0.0)
    terms = kaiser_coefficients()
    result = jnp.full_like(inside, terms[-1])
    for term in reversed(terms[:-1]):
        result = result * inside + term
    return result


def dft_tables(size):
    index = np.arange(size)
    angles = (index[:, None] * index[None, :] % size) * (2.0 * np.pi / size)
    cosine, sine = np.cos(angles), np.sin(angles)
    right = np.block([[cosine, sine], [-sine, cosine]])
    left = np.block([[cosine, -sine], [sine, cosine]])
    return right.astype(np.float32), left.astype(np.float32)


def write_message(samples_ref, density_ref, frac_ref, shift_ref, depth_ref, base_ref, out_ref, lines_ref):
    frames, blocks, channels, lanes = samples_ref.shape
    coils = channels // 2
    grid_mask = 127
    row = lax.broadcasted_iota(jnp.int32, (8, lanes), 0)
    offset = row.astype(jnp.float32)
    for frame in range(frames):
        for block in range(blocks):
            slot = frame * blocks + block
            lines_ref[slot] = samples_ref[frame, block].astype(jnp.float32) * density_ref[frame, block : block + 1].astype(jnp.float32)
            taps = [
                jnp.where(row < TAPS, kaiser(offset, frac_ref[frame, axis, block : block + 1].astype(jnp.float32)), 0.0)
                for axis in range(3)
            ]
            plane = base_ref[frame, 0, block].astype(jnp.float32)
            first_row = (shift_ref[frame, block : block + 1] + base_ref[frame, 1, block]) & grid_mask
            first_cell = depth_ref[frame, block : block + 1]
            group_x = jnp.where(row == ROW_XB - ROW_WX, plane, taps[0])
            group_y = jnp.where(row == ROW_YB - ROW_WY, first_row.astype(jnp.float32), taps[1])
            group_y = jnp.where(row == ROW_ZB - ROW_WY, first_cell.astype(jnp.float32), group_y)
            out_ref[frame, block, 0:coils] = lines_ref[slot, pl.ds(0, coils, stride=2), :].astype(jnp.bfloat16)
            out_ref[frame, block, coils:channels] = lines_ref[slot, pl.ds(1, coils, stride=2), :].astype(jnp.bfloat16)
            out_ref[frame, block, ROW_WX : ROW_WX + 16] = jnp.concatenate([group_x, taps[2]], axis=0).astype(jnp.bfloat16)
            out_ref[frame, block, ROW_WY : ROW_WY + 8] = group_y.astype(jnp.bfloat16)


def row_tables(rows, grid, lanes):
    image_rows = np.arange(grid).reshape(grid // rows, rows, 1)
    angles = (image_rows * np.arange(lanes) % grid) * (2.0 * np.pi / grid)
    cosine, sine = np.cos(angles), np.sin(angles)
    pairs = [(cosine, sine), (sine, cosine), (cosine, cosine), (-sine, sine)]
    return np.stack([np.concatenate(pair, axis=1) for pair in pairs], axis=1).astype(np.float32)


def gather_kernel(side, *refs):
    *input_refs, out_ref, msg_ref, lines_ref, send_sem, recv_sem, own_sem = refs
    tile = lax.axis_index("tile")
    core, chip = tile % 2, tile // 2
    chip_x, chip_y = chip // side, chip % side
    first = chip_x + core * (chip_y - chip_x)
    other = chip_y + core * (chip_x - chip_y)
    first_step = 2 * side - (2 * side - 2) * core
    other_step = 2 + (2 * side - 2) * core

    def at(along, across):
        return ((first + along + side) % side) * first_step + ((other + across + side) % side) * other_step + core

    partner = tile + 1 - 2 * core
    neighbours = [at(1, 0), at(-1, 0), at(2, 0), at(0, 1), at(0, -1), at(0, 2), partner]

    barrier = pltpu.get_barrier_semaphore()
    for device in neighbours:
        pl.semaphore_signal(barrier, inc=1, device_id={"tile": device}, device_id_type=MESH)
    write_message(*input_refs, msg_ref, lines_ref)
    pl.semaphore_wait(barrier, len(neighbours))

    copies = {}

    def make(key, slot, frame, target, own):
        number = len(copies)
        source = msg_ref if own else out_ref.at[slot]
        copies[key] = pltpu.make_async_remote_copy(
            src_ref=source if frame is None else source.at[frame],
            dst_ref=out_ref.at[slot] if frame is None else out_ref.at[slot, frame],
            send_sem=send_sem.at[number],
            recv_sem=recv_sem.at[number],
            device_id={"tile": target},
            device_id_type=MESH,
        )

    for frame in (0, 1):
        for way in (1, -1):
            make(("first", 0, frame, way), tile, frame, at(way, 0), True)
    make(("pass", 0), tile, 0, at(2, 0), True)
    make(("pass", 1), tile, 1, at(2, 0), True)
    for along in (0, -1, 1, 2):
        for frame in (0, 1):
            for way in (1, -1):
                make(("second", along, frame, way), at(along, 0), frame, at(0, way), along == 0)
        for frame in (0, 1):
            way = 1 - 2 * frame
            if along == 2:
                make(("hand", along, frame), at(along, 0), frame, at(0, 2), along == 0)
            else:
                make(("hand", along, frame), at(along, -way), frame, at(0, way), False)
        for across in (0, -1, 1, 2):
            make(("core", along, across), at(along, across), None, partner, along == 0 and across == 0)

    def start(*keys):
        for key in keys:
            copies[key].start()

    def arrived(*keys):
        for key in keys:
            copies[key].wait_recv()

    def second(along, *frames):
        for frame in frames:
            way = 1 - 2 * frame
            start(("second", along, frame, way), ("second", along, frame, -way))
            if along == 2:
                start(("hand", along, frame))

    there = {}

    def to_core(along, across, *frames):
        there[along, across] = there.get((along, across), 0) + len(frames)
        if there[along, across] == 2:
            start(("core", along, across))

    own = pltpu.make_async_copy(msg_ref, out_ref.at[tile], own_sem)
    start(("first", 0, 0, 1), ("first", 0, 1, -1), ("first", 0, 1, 1), ("first", 0, 0, -1), ("pass", 0), ("pass", 1))
    second(0, 0, 1)
    own.start()
    to_core(0, 0, 0, 1)
    arrived(("first", 0, 0, 1))
    second(-1, 0)
    to_core(-1, 0, 0)
    arrived(("first", 0, 1, -1))
    second(1, 1)
    to_core(1, 0, 1)
    arrived(("first", 0, 1, 1))
    second(-1, 1)
    to_core(-1, 0, 1)
    arrived(("first", 0, 0, -1))
    second(1, 0)
    to_core(1, 0, 0)
    arrived(("second", 0, 0, 1))
    start(("hand", 0, 0))
    to_core(0, -1, 0)
    arrived(("second", 0, 1, -1))
    start(("hand", 0, 1))
    to_core(0, 1, 1)
    arrived(("pass", 0))
    second(2, 0)
    to_core(2, 0, 0)
    arrived(("pass", 1))
    second(2, 1)
    to_core(2, 0, 1)
    arrived(("second", 0, 1, 1))
    to_core(0, -1, 1)
    arrived(("second", 0, 0, -1))
    to_core(0, 1, 0)
    for along in (-1, 1, 2):
        order = (0, 1) if along != 1 else (1, 0)
        for frame in order:
            way = 1 - 2 * frame
            arrived(("second", along, frame, way))
            if along != 2:
                start(("hand", along, frame))
            to_core(along, -way, frame)
        for frame in order:
            way = 1 - 2 * frame
            arrived(("second", along, frame, -way))
            to_core(along, way, frame)
    for along in (0, -1, 1, 2):
        for frame in (0, 1):
            arrived(("hand", along, frame))
            to_core(along, 2, frame)
    for key in [key for key in copies if key[0] == "core"]:
        copies[key].wait_recv()
    for copy in copies.values():
        copy.wait_send()
    own.wait()


def gather_messages(kspace_samples, density, sample_frac, row_offsets, depth_base, block_base, tiles):
    frames, blocks, channels, lanes = kspace_samples.shape
    message = (frames, blocks, ROWS, lanes)
    vmem, smem = pl.BlockSpec(memory_space=pltpu.VMEM), pl.BlockSpec(memory_space=pltpu.SMEM)
    return pl.pallas_call(
        functools.partial(gather_kernel, math.isqrt(tiles // 2)),
        out_shape=jax.ShapeDtypeStruct((tiles,) + message, jnp.bfloat16),
        in_specs=[vmem] * 5 + [smem],
        out_specs=pl.BlockSpec(memory_space=pl.ANY),
        scratch_shapes=[
            pltpu.VMEM(message, jnp.bfloat16),
            pltpu.VMEM((frames * blocks, channels, lanes), jnp.float32),
            pltpu.SemaphoreType.DMA((46,)),
            pltpu.SemaphoreType.DMA((46,)),
            pltpu.SemaphoreType.DMA(()),
        ],
        compiler_params=pltpu.CompilerParams(collective_id=0, has_side_effects=True),
        name="gather",
    )(kspace_samples, density, jnp.swapaxes(sample_frac, 1, 2), row_offsets, depth_base, jnp.swapaxes(block_base, 1, 2))


def grid_kernel(grid, coils, rows, blocks, scale, tile_ref, msg_hbm, tables_hbm, right_ref, left_ref, maps_hbm, est_hbm, out_ref, sent_ref, acc_ref, steps_ref, lines_ref, msg_ref, tables_ref, maps_ref, est_ref, msg_sem, tables_sem, maps_sem, est_sem):
    frame = pl.program_id(0)
    half_rows = rows * coils

    def message_copy(which):
        return pltpu.make_async_copy(msg_hbm.at[:, which], msg_ref.at[which], msg_sem.at[which])

    tables_copy = pltpu.make_async_copy(tables_hbm.at[tile_ref[0]], tables_ref, tables_sem)
    maps_copy = pltpu.make_async_copy(maps_hbm, maps_ref, maps_sem)
    est_copy = pltpu.make_async_copy(est_hbm, est_ref, est_sem)

    @pl.when(frame == 0)
    def _():
        tables_copy.start()
        for which in range(2):
            message_copy(which).start()
        maps_copy.start()
        est_copy.start()

    plane = 2 * half_rows
    per_tile = msg_ref.shape[2]
    pitch = plane + 8

    def clear(step, carry):
        acc_ref[pl.ds(pl.multiple_of(step * 128, 128), 128), :] = jnp.zeros((128, grid), jnp.float32)
        return carry

    lax.fori_loop(0, grid * pitch // 128, clear, 0, unroll=4)
    @pl.when(frame == 0)
    def _():
        tables_copy.wait()

    message_copy(frame).wait()
    for tap in range(TAPS):
        steps_ref[tap] = jnp.broadcast_to(tables_ref[2][:, tap : tap + 1], (2 * rows, 128))
        steps_ref[TAPS + tap] = jnp.broadcast_to(tables_ref[3][:, tap : tap + 1], (2 * rows, 128))
    cells = lax.broadcasted_iota(jnp.int32, (8, 128), 0)

    def one_block(block, carry):
        tile, local = block // per_tile, block % per_tile
        real = msg_ref[frame, tile, local, 0:coils, :].astype(jnp.float32)
        imag = msg_ref[frame, tile, local, coils : 2 * coils, :].astype(jnp.float32)
        weights = msg_ref[frame, tile, local, ROW_WX : ROW_WX + 8, :].astype(jnp.float32)
        depth = msg_ref[frame, tile, local, ROW_WZ : ROW_WZ + 8, :].astype(jnp.float32)
        tail = msg_ref[frame, tile, local, ROW_WY : ROW_WY + 8, :].astype(jnp.float32)
        first_row = jnp.broadcast_to(tail[ROW_YB - ROW_WY : ROW_YB - ROW_WY + 1, :].astype(jnp.int32), (8, 128))
        first_cell = tail[ROW_ZB - ROW_WY : ROW_ZB - ROW_WY + 1, :].astype(jnp.int32)
        turn = jnp.take_along_axis(tables_ref[0], first_row, axis=1)
        swapped = jnp.take_along_axis(tables_ref[1], first_row, axis=1)
        sum_same = sum(tail[e : e + 1] * steps_ref[e] for e in range(TAPS))
        sum_cross = sum(tail[e : e + 1] * steps_ref[TAPS + e] for e in range(TAPS))
        phase = turn * sum_same + swapped * sum_cross
        reals = [real * phase[y : y + 1] - imag * phase[rows + y : rows + y + 1] for y in range(rows)]
        imags = [real * phase[rows + y : rows + y + 1] + imag * phase[y : y + 1] for y in range(rows)]
        field = jnp.concatenate(reals + imags, axis=0)
        low = cells - (first_cell & 15)
        inside = [jnp.take_along_axis(depth, jnp.minimum((low + part) & 31, 7), axis=0) for part in (0, 8)]
        after = [jnp.take_along_axis(depth, jnp.minimum(low + part, 7), axis=0) for part in (16, 24)]
        inside = jnp.concatenate(inside, axis=0).astype(jnp.bfloat16)
        after = jnp.concatenate(after, axis=0).astype(jnp.bfloat16)
        group = jnp.broadcast_to((first_cell >> 4).astype(jnp.float32), (16, 128)).astype(jnp.bfloat16)
        hits = [group == jnp.asarray(index, jnp.bfloat16) for index in range(grid // 16)]
        nothing = jnp.zeros((16, 128), jnp.bfloat16)
        spread = jnp.concatenate(
            [jnp.where(hits[index], inside, jnp.where(hits[index - 1], after, nothing)) for index in range(grid // 16)], axis=0
        )
        field16 = field.astype(jnp.bfloat16).reshape(plane // 16, 16, 128)
        left = jnp.concatenate(
            [field16 * jnp.broadcast_to(weights[tap : tap + 1], (16, 128)).astype(jnp.bfloat16)[None] for tap in range(TAPS)], axis=0
        ).reshape(TAPS * plane, 128)
        value = lax.dot_general(left, spread, (((1,), (1,)), ((), ())), preferred_element_type=jnp.float32)
        first_plane = weights[ROW_XB - ROW_WX : ROW_XB - ROW_WX + 1, :].astype(jnp.int32)[0, 0]
        for tap in range(TAPS):
            start = pl.multiple_of(((first_plane + tap) & (grid - 1)) * pitch, 8)
            acc_ref[pl.ds(start, plane), :] += value[tap * plane : (tap + 1) * plane]
        return carry

    lax.fori_loop(0, blocks, one_block, 0, unroll=64)

    @pl.when(frame == 0)
    def _():
        maps_copy.wait()
        est_copy.wait()

    right = right_ref[...]
    left = left_ref[...]
    for y in range(rows):
        out_ref[0, 0, y] = jnp.zeros((grid, grid), jnp.float32)
        out_ref[0, 1, y] = jnp.zeros((grid, grid), jnp.float32)

        for group in range(0, coils, 4):
            lines = []
            for coil in range(group, group + 4):
                base = y * coils + coil
                re = acc_ref[pl.ds(base, grid, stride=pitch), :]
                im = acc_ref[pl.ds(half_rows + base, grid, stride=pitch), :]
                lines.append(jnp.concatenate([re, im], axis=1).astype(jnp.bfloat16))
            lines_ref[group * grid : (group + 4) * grid] = jnp.dot(
                jnp.concatenate(lines, axis=0), right, preferred_element_type=jnp.float32
            ).astype(jnp.bfloat16)

        def one_pair(pair, carry, y=y):
            coil = pair * 2
            first_line = pl.multiple_of(coil * grid, 2 * grid)
            one, two = lines_ref[pl.ds(first_line, grid)], lines_ref[pl.ds(first_line + grid, grid)]
            stacked = jnp.concatenate(
                [
                    jnp.concatenate([one[:, :grid], two[:, :grid]], axis=1),
                    jnp.concatenate([one[:, grid:], two[:, grid:]], axis=1),
                ],
                axis=0,
            )
            image = jnp.dot(left, stacked, preferred_element_type=jnp.float32)
            back_re = jnp.zeros((grid, grid), jnp.float32)
            back_im = jnp.zeros((grid, grid), jnp.float32)
            for part in range(2):
                image_re = image[:grid, part * grid : (part + 1) * grid]
                image_im = image[grid:, part * grid : (part + 1) * grid]
                map_re = maps_ref[coil + part, 0, y].astype(jnp.float32)
                map_im = maps_ref[coil + part, 1, y].astype(jnp.float32)
                back_re += map_re * image_re + map_im * image_im
                back_im += map_re * image_im - map_im * image_re
            out_ref[0, 0, y] += back_re
            out_ref[0, 1, y] += back_im
            return carry

        lax.fori_loop(0, coils // 2, one_pair, 0, unroll=8)
        for part in range(2):
            half = est_ref[frame, part, y] + scale * out_ref[0, part, y]
            out_ref[0, part, y] = half
            sent_ref[0, part, y] = half.astype(jnp.bfloat16)


def half_step(gathered, tile, coil_maps, estimate, scale):
    tiles, frames, per_tile = gathered.shape[:3]
    coils, _, rows, grid, _ = coil_maps.shape
    blocks = tiles * per_tile
    right, left = (jnp.asarray(table, jnp.bfloat16) for table in dft_tables(grid))
    tables = jnp.asarray(row_tables(rows, grid, gathered.shape[-1]))
    once, anywhere = pl.Buffered(1), pl.BlockSpec(memory_space=pl.ANY)
    return pl.pallas_call(
        functools.partial(grid_kernel, grid, coils, rows, blocks, scale),
        out_shape=[jax.ShapeDtypeStruct(estimate.shape, kind) for kind in (jnp.float32, jnp.bfloat16)],
        grid_spec=pltpu.PrefetchScalarGridSpec(
            num_scalar_prefetch=1,
            grid=(frames,),
            in_specs=[
                anywhere,
                anywhere,
                pl.BlockSpec((2 * grid, 2 * grid), lambda f, s: (0, 0), pipeline_mode=once),
                pl.BlockSpec((2 * grid, 2 * grid), lambda f, s: (0, 0), pipeline_mode=once),
                anywhere,
                anywhere,
            ],
            out_specs=[pl.BlockSpec((1, 2, rows, grid, grid), lambda f, s: (f, 0, 0, 0, 0))] * 2,
            scratch_shapes=[
                pltpu.VMEM((grid * (2 * rows * coils + 8), grid), jnp.float32),
                pltpu.VMEM((2 * TAPS, 2 * rows, 128), jnp.float32),
                pltpu.VMEM((coils * grid, 2 * grid), jnp.bfloat16),
                pltpu.VMEM((frames, tiles, per_tile, ROWS, 128), gathered.dtype),
                pltpu.VMEM(tables.shape[1:], tables.dtype),
                pltpu.VMEM(coil_maps.shape, coil_maps.dtype),
                pltpu.VMEM(estimate.shape, estimate.dtype),
                pltpu.SemaphoreType.DMA((frames,)),
                pltpu.SemaphoreType.DMA(()),
                pltpu.SemaphoreType.DMA(()),
                pltpu.SemaphoreType.DMA(()),
            ],
        ),
        compiler_params=pltpu.CompilerParams(vmem_limit_bytes=56 * 1024 * 1024),
        name="grid",
    )(tile, gathered, tables, right, left, coil_maps, estimate)


def exchange_kernel(count, half_ref, before_ref, after_ref, send_sem, recv_sem):
    here = lax.axis_index("frame")
    upper, lower = (here + 1) % count, (here + count - 1) % count
    barrier = pltpu.get_barrier_semaphore()
    for device in (upper, lower):
        pl.semaphore_signal(barrier, inc=1, device_id={"frame": device}, device_id_type=MESH)
    pl.semaphore_wait(barrier, 2)
    copies = [
        pltpu.make_async_remote_copy(
            src_ref=half_ref.at[frame],
            dst_ref=target,
            send_sem=send_sem.at[number],
            recv_sem=recv_sem.at[number],
            device_id={"frame": device},
            device_id_type=MESH,
        )
        for number, (frame, target, device) in enumerate(
            [(half_ref.shape[0] - 1, before_ref, upper), (0, after_ref, lower)]
        )
    ]
    for copy in copies:
        copy.start()
    for copy in copies:
        copy.wait()


def exchange_frames(half, count):
    anywhere = pl.BlockSpec(memory_space=pl.ANY)
    return pl.pallas_call(
        functools.partial(exchange_kernel, count),
        out_shape=[jax.ShapeDtypeStruct(half.shape[1:], half.dtype)] * 2,
        in_specs=[anywhere],
        out_specs=[anywhere] * 2,
        scratch_shapes=[pltpu.SemaphoreType.DMA((2,)), pltpu.SemaphoreType.DMA((2,))],
        compiler_params=pltpu.CompilerParams(collective_id=1, has_side_effects=True),
        name="exchange",
    )(half)


def variation_kernel(count, frame_ref, half_ref, before_ref, after_ref, out_ref):
    here = frame_ref[0]

    def psi(later, earlier):
        change = [later[part] - earlier[part] for part in range(2)]
        factor = lax.rsqrt(change[0] * change[0] + change[1] * change[1] + EPS * EPS)
        return [change[part] * factor for part in range(2)]

    for y in range(half_ref.shape[2]):
        first = [half_ref[0, part, y] for part in range(2)]
        last = [half_ref[1, part, y] for part in range(2)]
        before = [before_ref[part, y].astype(jnp.float32) for part in range(2)]
        after = [after_ref[part, y].astype(jnp.float32) for part in range(2)]
        psi_before, psi_here, psi_after = psi(first, before), psi(last, first), psi(after, last)
        for part in range(2):
            low = jnp.where(here > 0, psi_before[part], 0.0)
            high = jnp.where(here < count - 1, psi_after[part], 0.0)
            out_ref[0, part, y] = first[part] - LAMBDA_TV * (low - psi_here[part])
            out_ref[1, part, y] = last[part] - LAMBDA_TV * (psi_here[part] - high)


def variation_step(half, before, after, frame_here, count):
    frames, parts, rows, grid, _ = half.shape
    assert frames == 2
    whole = pl.BlockSpec((frames, parts, rows // 2, grid, grid), lambda y, s: (0, 0, y, 0, 0))
    side = pl.BlockSpec((parts, rows // 2, grid, grid), lambda y, s: (0, y, 0, 0))
    return pl.pallas_call(
        functools.partial(variation_kernel, count),
        out_shape=jax.ShapeDtypeStruct(half.shape, half.dtype),
        grid_spec=pltpu.PrefetchScalarGridSpec(
            num_scalar_prefetch=1, grid=(2,), in_specs=[whole, side, side], out_specs=whole
        ),
        name="variation",
    )(frame_here, half, before, after)


def on_device(
    kspace_samples, density, sample_frac, row_offsets, depth_base, block_base, coil_maps, estimate
):
    tile_count = lax.axis_size("tile")
    tile_here = lax.axis_index("tile")
    frame_here = lax.axis_index("frame")
    frames, per_tile, channels, samples = kspace_samples.shape
    coils = channels // 2
    grid = coil_maps.shape[3]
    rows = coil_maps.shape[2]
    scale = 1.0 / (8.0 * math.sqrt(per_tile * tile_count * samples))

    gathered = gather_messages(
        kspace_samples, density, sample_frac, row_offsets, depth_base, block_base, tile_count
    )
    half, rounded = half_step(gathered, tile_here.reshape(1), coil_maps, estimate, scale)
    before, after = exchange_frames(rounded, lax.axis_size("frame"))
    return variation_step(half, before, after, frame_here.reshape(1), lax.axis_size("frame"))


def solution(mesh):
    in_specs = (
        P("frame", "tile", None, None),
        P("frame", "tile", None),
        P("frame", "tile", None, None),
        P("frame", "tile", None),
        P("frame", "tile", None),
        P("frame", "tile", None),
        P(None, None, "tile", None, None),
        P("frame", None, "tile", None, None),
    )
    out_specs = P("frame", None, "tile", None, None)
    return jax.shard_map(
        on_device, mesh=mesh, in_specs=in_specs, out_specs=out_specs, check_vma=False
    )
```
